512 devices in a mesh: blk: 128 (over z, y, core), head: 4 (over x).
Axes of the slice: x: 4, y: 8, z: 8, core: 2. Of those that a mesh axis runs over, the one named last changes fastest.
Arguments:
- hidden_in: bfloat16 [512, 1024], P('blk'), may hold values from -6 to 6
- norm_gain: float32 [1024], replicated, may hold values from 0.25 to 1.75
- w_query: bfloat16 [1024, 1024], P(None, 'head'), may hold values from -0.1875 to 0.1875
- w_key: bfloat16 [1024, 1024], P(None, 'head'), may hold values from -0.1875 to 0.1875
- w_value: bfloat16 [1024, 1024], P(None, 'head'), may hold values from -0.1875 to 0.1875
- w_out: bfloat16 [1024, 1024], P('head'), may hold values from -0.1875 to 0.1875
- cache_keys: bfloat16 [256, 128, 1024], P('blk', None, 'head'), may hold values from -30 to 30
- cache_values: bfloat16 [256, 128, 1024], P('blk', None, 'head'), may hold values from -6 to 6
- block_node: int32 [256], P('blk'), may hold values from 0 to 167
- block_len: int32 [256], P('blk'), may hold values from 1 to 128, as said below
- live_count: int32 [128], P('blk'), may hold values from 1 to 2, as said below
- node_parent: int32 [168], replicated, may hold values from -1 to 39, as said below
- request_leaf: int32 [512], replicated, may hold values from 40 to 167
Outputs:
- hidden_out: bfloat16 [512, 1024], P('blk', 'head')
- new_keys: bfloat16 [512, 1024], P('blk', 'head')
- new_values: bfloat16 [512, 1024], P('blk', 'head')
The draws below stay inside these ranges and needn't reach their ends.
Inputs may be any that keep to these rules, and one draw needn't show every extreme that they name: `block_len`: some block of every draw is full. `live_count`: some index of blk uses all its slots in every draw. `node_parent`: nodes 0 to 7 are roots (parent -1); a node of ids 8 to 39 has a root as parent; every later node has a second-level parent.
All inputs are finite; a program needn't handle non-finite values.
Results may differ from the reference program's by a relative error of at most 0.012.
The reference program's roundings to bfloat16 on the way (of `normed` and `attended`) count: a program that leaves them out, or rounds other values in their place, can miss the bound.
Values may be sent and summed in bfloat16 or wider, within the bound.
A program may use at most 64 MiB of HBM per device.

```python
import jax
import jax.numpy as jnp
from jax import lax

D = 1024
H = 16
HD = 64
BT = 128
BLK_DEV = 2
N_ROOT = 8
N_MID = 32
NODES = 168
R = 512
SLOTS = 256


def draw_cache_keys(key, part):
    base = jnp.clip(jax.random.normal(key, (SLOTS, BT, H * HD), jnp.float32), -6.0, 6.0)
    return base.astype(jnp.bfloat16)


def draw_block_len(key, part):
    groups = SLOTS // BLK_DEV
    lengths = jax.random.randint(key, (SLOTS,), 1, BT + 1)
    chosen = jax.random.randint(jax.random.fold_in(key, 5), (), 0, groups)
    slots = jnp.arange(SLOTS, dtype=jnp.int32)
    return jnp.where(slots == chosen * BLK_DEV, BT, lengths).astype(jnp.int32)


def draw_live_count(key, part):
    groups = SLOTS // BLK_DEV
    base = jax.random.randint(key, (groups,), 0, BLK_DEV)
    counts = 1 + base * base // BLK_DEV
    chosen = jax.random.randint(jax.random.fold_in(key, 3), (), 0, groups)
    return jnp.where(jnp.arange(groups, dtype=jnp.int32) == chosen, BLK_DEV, counts).astype(jnp.int32)


def draw_node_parent(key, part):
    node_ids = jnp.arange(NODES, dtype=jnp.int32)
    mid_parent = jax.random.randint(key, (NODES,), 0, N_ROOT)
    leaf_parent = jax.random.randint(jax.random.fold_in(key, 5), (NODES,), N_ROOT, N_ROOT + N_MID)
    return jnp.where(node_ids < N_ROOT, -1, jnp.where(node_ids < N_ROOT + N_MID, mid_parent, leaf_parent)).astype(jnp.int32)


def place_ends(values, own_key, low, high):
    longest = values.shape.index(max(values.shape))
    spots = []
    for shift in (0, 1):
        where = [jax.random.randint(jax.random.fold_in(own_key, axis), (), 0, length) for axis, length in enumerate(values.shape)]
        where[longest] = (where[longest] + shift) % values.shape[longest]
        spots.append(tuple(where))
    return values.at[spots[0]].set(low).at[spots[1]].set(high)


def steps_of(own_key, extent, pieces, smallest, top_value):
    def one(position, parts):
        heights = jax.random.uniform(jax.random.fold_in(jax.random.fold_in(own_key, 6), position), (parts,), jnp.float32, smallest / len(pieces), top_value / len(pieces))
        return jnp.repeat(jnp.exp(heights), extent[position] // parts).reshape((-1,) + (1,) * (len(extent) - position - 1))

    loudness = one(*pieces[0])
    for cut in pieces[1:]:
        loudness = loudness * one(*cut)
    return loudness


def bell_draw(own_key, extent, scale, most, pieces=(), kind=jnp.bfloat16):
    drawn = scale * jax.random.normal(own_key, extent, jnp.float32)
    if pieces:
        drawn = drawn * steps_of(own_key, extent, pieces, -0.22, 0.18)
    return jnp.clip(drawn, -most, most).astype(kind)


def setup_inputs(seed: int = 0) -> dict:
    streams_of = jax.random.split(jax.random.key(seed), 14)
    return {
        "hidden_in": bell_draw(streams_of[0], (R, D), 1.0, 6.0, ((0, 128),)),
        "norm_gain": jnp.clip(1.0 + 0.15 * jax.random.normal(streams_of[1], (D,), jnp.float32), 0.25, 1.75),
        "w_query": bell_draw(streams_of[2], (D, H * HD), D ** -0.5, 0.1875, ((1, 4),)),
        "w_key": bell_draw(streams_of[3], (D, H * HD), D ** -0.5, 0.1875, ((1, 4),)),
        "w_value": bell_draw(streams_of[4], (D, H * HD), D ** -0.5, 0.1875, ((1, 4),)),
        "w_out": bell_draw(streams_of[5], (H * HD, D), (H * HD) ** -0.5, 0.1875, ((0, 4),)),
        "cache_keys": draw_cache_keys(jax.random.fold_in(streams_of[13], 71), 0),
        "cache_values": bell_draw(streams_of[7], (SLOTS, BT, H * HD), 1.0, 6.0, ((0, 128), (2, 4))),
        "block_node": place_ends(jax.random.randint(streams_of[8], (SLOTS,), 0, NODES), jax.random.fold_in(streams_of[8], 1), 0, NODES - 1).astype(jnp.int32),
        "block_len": draw_block_len(jax.random.fold_in(streams_of[13], 71), 0),
        "live_count": draw_live_count(jax.random.fold_in(streams_of[13], 71), 0),
        "node_parent": draw_node_parent(jax.random.fold_in(streams_of[13], 71), 0),
        "request_leaf": place_ends(jax.random.randint(streams_of[12], (R,), N_ROOT + N_MID, NODES), jax.random.fold_in(streams_of[12], 1), N_ROOT + N_MID, NODES - 1).astype(jnp.int32),
    }


very_low = -1e+30

def reference(hidden_in, norm_gain, w_query, w_key, w_value, w_out, cache_keys, cache_values, block_node, block_len, live_count, node_parent, request_leaf):
    states = hidden_in.astype(jnp.float32)
    scale_inv = lax.rsqrt(lax.optimization_barrier(jnp.mean(states * states, axis=1, keepdims=True)) + 1e-06)
    normed = (states * scale_inv * norm_gain[None, :]).astype(jnp.bfloat16)
    query = jnp.dot(normed, w_query, preferred_element_type=jnp.float32).astype(jnp.bfloat16)
    key_new = jnp.dot(normed, w_key, preferred_element_type=jnp.float32).astype(jnp.bfloat16)
    value_new = jnp.dot(normed, w_value, preferred_element_type=jnp.float32).astype(jnp.bfloat16)
    rows = states.shape[0]
    query_four = query.reshape(rows, H, HD).astype(jnp.float32)
    first = node_parent[request_leaf]
    second = node_parent[first]
    path = jnp.stack([request_leaf, first, second], axis=1)
    groups = cache_keys.shape[0] // BLK_DEV
    keys_grouped = cache_keys.reshape(groups, BLK_DEV, BT, H, HD)
    values_grouped = cache_values.reshape(groups, BLK_DEV, BT, H, HD)
    nodes_grouped = block_node.reshape(groups, BLK_DEV)
    lens_grouped = block_len.reshape(groups, BLK_DEV)
    slot_ids = jnp.arange(BLK_DEV, dtype=jnp.int32)
    positions = jnp.arange(BT, dtype=jnp.int32)

    def masked(group):
        keys, values, nodes, lens, count = group
        scores = jnp.einsum('rhd,sthd->rhst', query_four, keys.astype(jnp.float32))
        seen = jnp.any(path[:, :, None] == nodes[None, None, :], axis=1) & (slot_ids < count)[None, :]
        valid = seen[:, :, None] & (positions[None, :] < lens[:, None])[None, :, :]
        return (jnp.where(valid[:, None], scores, very_low), valid, values)
    own_score = lax.optimization_barrier(jnp.sum(query_four * key_new.reshape(rows, H, HD).astype(jnp.float32), axis=2))
    stacked = (keys_grouped, values_grouped, nodes_grouped, lens_grouped, live_count)

    def max_step(carry, group):
        scores, valid, values = masked(group)
        return (jnp.maximum(carry, lax.optimization_barrier(jnp.max(scores, axis=(2, 3)))), None)
    top, unused = lax.scan(max_step, own_score, stacked)

    def sum_step(carry, group):
        denom, numer = carry
        scores, valid, values = masked(group)
        weights = jnp.where(valid[:, None], jnp.exp(scores - top[:, :, None, None]), 0.0)
        rounded = lax.optimization_barrier(weights.astype(jnp.bfloat16)).astype(jnp.float32)
        denom = denom + lax.optimization_barrier(jnp.sum(weights, axis=(2, 3)))
        numer = numer + jnp.einsum('rhst,sthd->rhd', rounded, values.astype(jnp.float32))
        return ((denom, numer), None)
    start = (jnp.zeros((rows, H), jnp.float32), jnp.zeros((rows, H, HD), jnp.float32))
    (denom, numer), unused = lax.scan(sum_step, start, stacked)
    own_weight = jnp.exp(own_score - top)
    denom = denom + own_weight
    own_round = lax.optimization_barrier(own_weight.astype(jnp.bfloat16)).astype(jnp.float32)
    numer = numer + own_round[:, :, None] * value_new.reshape(rows, H, HD).astype(jnp.float32)
    attended = (numer / denom[:, :, None]).reshape(rows, H * HD).astype(jnp.bfloat16)
    hidden_out = (states + jnp.dot(attended, w_out, preferred_element_type=jnp.float32)).astype(jnp.bfloat16)
    return (hidden_out, key_new, value_new)
```

```python
import functools
import math

import jax
import jax.numpy as jnp
from jax import lax
from jax.experimental import pallas as pl
from jax.experimental.pallas import tpu as pltpu
from jax.sharding import PartitionSpec as P

HD = 64
RD = 4
BT = 128
SL = 2
W = 128
MESH = pl.DeviceIdType.MESH
F32 = jnp.float32
BF16 = jnp.bfloat16

very_low = -1e30
low_top = -1e29


def iota(shape, axis):
    return lax.broadcasted_iota(jnp.int32, shape, axis)


def dot_nt(a, b):
    return lax.dot_general(a, b, (((1,), (1,)), ((), ())), preferred_element_type=F32)


def dot(a, b):
    return jnp.dot(a, b, preferred_element_type=F32)


def kernel(
    side,
    heads_n,
    hidden_h,
    gain_h,
    parent_h,
    leaf_h,
    node_h,
    len_h,
    live_h,
    wq_h,
    wk_h,
    wv_h,
    wo_h,
    ck_h,
    cv_h,
    out,
    out_k,
    out_v,
    hidden,
    gain,
    parent,
    leaf,
    node,
    length,
    live,
    wq,
    wk,
    wv,
    wo,
    kbuf,
    vbuf,
    vt,
    hid8,
    g1,
    g2,
    meta_send,
    meta_recv,
    par,
    lim,
    r2s,
    r2,
    r3s,
    r3,
    xs,
    xr,
    res,
    lsem,
    csem,
    crem,
    g1s_sem,
    g1r_sem,
    g2s_sem,
    g2r_sem,
    r2s_sem,
    r2r_sem,
    r3s_sem,
    r3r_sem,
    xs_sem,
    xr_sem,
):
    n = side
    rows = n * 2 * RD
    lanes = 2 * rows
    nodes = par.shape[1]
    total = leaf.shape[1]
    me = lax.axis_index("blk")
    hd = lax.axis_index("head")
    core = me % 2
    y = (me // 2) % n
    z = me // (2 * n)
    flip = 1 - core
    a = y * flip + z * core
    b = z * flip + y * core

    def device(aa, bb, cc, hh):
        zz = bb * flip + aa * core
        yy = aa * flip + bb * core
        return {"blk": (zz * n + yy) * 2 + cc, "head": hh}

    def along_a(k):
        return device((a + k + n) % n, b, core, hd)

    def along_b(k):
        return device(a, (b + k + n) % n, core, hd)

    def along_x(k):
        return {"blk": me, "head": (hd + k) % heads_n}

    other = {"blk": me + 1 - 2 * core, "head": hd}

    barrier = pltpu.get_barrier_semaphore()
    for k in range(1, n):
        pl.semaphore_signal(barrier, inc=1, device_id=along_b(k), device_id_type=MESH)
    for k in range(1, n):
        pl.semaphore_signal(barrier, inc=1, device_id=along_a(k), device_id_type=MESH)
    pl.semaphore_signal(barrier, inc=1, device_id=other, device_id_type=MESH)
    for k in range(1, heads_n):
        pl.semaphore_signal(barrier, inc=1, device_id=along_x(k), device_id_type=MESH)

    loads = [
        pltpu.make_async_copy(src, dst, lsem.at[k])
        for k, (src, dst) in enumerate(
            [
                (hidden_h, hidden),
                (gain_h, gain),
                (wq_h, wq),
                (node_h, node),
                (len_h, length),
                (live_h, live),
                (wk_h, wk),
                (wv_h, wv),
                (cv_h, vbuf.at[pl.ds(0, SL)]),
                (ck_h, kbuf.at[pl.ds(0, SL)]),
                (parent_h, parent),
                (leaf_h, leaf),
                (wo_h, wo),
            ]
        )
    ]
    for load in loads:
        load.start()

    loads[0].wait()
    loads[1].wait()
    states = hidden[...].astype(F32)
    hid8[pl.ds(0, RD), :] = states
    hid8[pl.ds(RD, RD), :] = states
    h8 = hid8[...]
    inv = lax.rsqrt(jnp.mean(h8 * h8, axis=1, keepdims=True) + 1e-06)
    normed = (h8 * inv * gain[...]).astype(BF16)
    row8 = iota((2 * RD, W), 0)
    lane8 = iota((2 * RD, W), 1)
    upper = row8 < RD

    def tile_of(wide):
        return jnp.where(upper, wide[:, 0:W], wide[:, W : 2 * W])

    loads[2].wait()
    q8 = tile_of(dot(normed, wq[...]).astype(BF16).astype(F32))
    g1[0] = q8

    for k in (3, 4, 5):
        loads[k].wait()
    own_len = [jnp.where(s < live[:, 0:1], length[:, s : s + 1], 0).astype(F32) for s in range(SL)]
    own_node = [node[:, s : s + 1].astype(F32) for s in range(SL)]

    def slot_tile(first):
        tile = jnp.zeros((8, W), F32)
        for s in range(SL):
            tile = jnp.where(row8 == first + s, own_node[s], tile)
            tile = jnp.where(row8 == 4 + first + s, own_len[s], tile)
        return tile

    meta_send[...] = slot_tile(SL)

    sends = []

    def send(src, dst, send_sem, recv_sem, target):
        copy = pltpu.make_async_remote_copy(
            src_ref=src,
            dst_ref=dst,
            send_sem=send_sem,
            recv_sem=recv_sem,
            device_id=target,
            device_id_type=MESH,
        )
        copy.start()
        sends.append(copy)
        return copy

    pl.semaphore_wait(barrier, 2 * (n - 1) + 1 + heads_n - 1)

    order = sorted(range(1, n), key=lambda k: -min(k, n - k))
    got1 = {k: send(g1.at[0], g1.at[k], g1s_sem.at[k], g1r_sem.at[k], along_b(k)) for k in order}
    got_meta = send(meta_send, meta_recv, csem.at[0], crem.at[0], other)
    got_v = send(cv_h, vbuf.at[pl.ds(SL, SL)], csem.at[1], crem.at[1], other)
    got_k = send(ck_h, kbuf.at[pl.ds(SL, SL)], csem.at[2], crem.at[2], other)

    loads[6].wait()
    k8 = dot(normed, wk[...]).astype(BF16)
    out_k[...] = k8[0:RD, :]
    loads[7].wait()
    v8 = dot(normed, wv[...]).astype(BF16)
    out_v[...] = v8[0:RD, :]
    k8 = tile_of(k8.astype(F32))
    v8 = tile_of(v8.astype(F32))
    prod = q8 * k8
    left = lane8 < HD
    own = jnp.where(
        left,
        jnp.sum(jnp.where(left, prod, 0.0), axis=1, keepdims=True),
        jnp.sum(jnp.where(left, 0.0, prod), axis=1, keepdims=True),
    )
    for k in range(heads_n):
        res[k] = tile_of(h8[:, 2 * W * k : 2 * W * (k + 1)])

    for k in range(1, n):
        got1[k].wait_recv()
    g2[0] = g1[...].reshape(rows, W).astype(BF16)
    got2 = {k: send(g2.at[0], g2.at[k], g2s_sem.at[k], g2r_sem.at[k], along_a(k)) for k in order}

    loads[10].wait()
    loads[11].wait()
    par[...] = jnp.full_like(par, -1.0)
    par[:, 0 : parent.shape[1]] = parent[...].astype(F32)
    node_of_row = iota((nodes, 1), 0).astype(F32)
    hop = jnp.where(node_of_row == par[...], 1.0, 0.0).astype(BF16)
    leaf_hot = jnp.where(node_of_row == leaf[...].astype(F32), 1.0, 0.0).astype(BF16)
    spot = iota((1, n * lanes), 1)
    at_i = lax.rem(a + n - spot // lanes, n)
    at_j = lax.rem(b + n - lax.rem(spot // (2 * RD), n), n)
    at_z = at_j * flip + at_i * core
    at_y = at_i * flip + at_j * core
    request = ((at_z * n + at_y) * 2 + core) * RD + lax.rem(spot, RD)
    pick = jnp.where(iota((total, 1), 0) == request, 1.0, 0.0).astype(BF16)

    got_meta.wait_recv()
    slots = slot_tile(0) + meta_recv[...]
    slot_node = jnp.concatenate([slots] * (nodes // W), axis=1)
    slot_len = jnp.concatenate([pltpu.roll(slots, 4, 0)] * (nodes // W), axis=1)
    level = jnp.where(iota((8, nodes), 1).astype(F32) == slot_node, 1.0, 0.0)
    up1 = dot(level.astype(BF16), hop)
    up2 = dot(up1.astype(BF16), hop)
    limits = ((level + up1 + up2) * slot_len).astype(BF16)
    limits = dot(limits, leaf_hot).astype(BF16)
    lim[...] = dot(limits, pick)

    loads[8].wait()
    got_v.wait_recv()
    vt[...] = vbuf[...].reshape(2 * SL * BT, 2 * W).astype(F32).T.astype(BF16)
    loads[9].wait()
    got_k.wait_recv()
    keys = kbuf[...].reshape(2 * SL * BT, 2 * W)

    spread_row = iota((lanes, 2 * W), 0)
    spread_lane = iota((lanes, 2 * W), 1)
    spread = jnp.where(
        (spread_row // rows == lax.rem(spread_lane // HD, 2)) & (lax.rem(spread_row // RD, 2) == spread_lane // W),
        1.0,
        0.0,
    ).astype(BF16)
    lane1 = iota((1, lanes), 1)
    lane_head = 2 * lax.rem(lane1 // RD, 2) + lane1 // rows
    token = iota((BT, lanes), 0).astype(F32)
    row16 = iota((16, lanes), 0)

    def partial(k):
        block = g2[k]
        block = jnp.concatenate([block, block], axis=1)
        queries = jnp.concatenate([block, block], axis=0) * spread
        scores = dot_nt(keys, queries)
        parts = []
        for s in range(2 * SL):
            limit = lim[s : s + 1, k * lanes : (k + 1) * lanes]
            parts.append(jnp.where(token < limit, scores[s * BT : (s + 1) * BT], very_low))
        masked = jnp.concatenate(parts, axis=0)
        top = jnp.maximum(jnp.max(masked, axis=0, keepdims=True), low_top)
        top_hi = top.astype(BF16).astype(F32)
        top_lo = (top - top_hi).astype(BF16).astype(F32)
        weights = jnp.exp(masked - (top_hi + top_lo))
        denom = jnp.sum(weights, axis=0, keepdims=True)
        full = dot(vt[...], weights.astype(BF16))
        numer = full[0:HD]
        for h in range(1, 4):
            numer = jnp.where(lane_head == h, full[h * HD : (h + 1) * HD], numer)
        den_hi = denom.astype(BF16).astype(F32)
        den_lo = denom - den_hi
        stats = jnp.where(
            row16 == 0,
            top_hi,
            jnp.where(row16 == 1, top_lo, jnp.where(row16 == 2, den_hi, den_lo)),
        )
        return numer.astype(BF16), stats.astype(BF16)

    got3 = {}
    for k in [0] + order[::-1]:
        if k:
            got2[k].wait_recv()
        numer, stats = partial(k)
        target = r2s.at[k] if k else r2.at[0]
        target[0:HD, :] = numer
        target[HD : HD + 16, :] = stats
        if k:
            got3[k] = send(r2s.at[k], r2.at[k], r2s_sem.at[k], r2r_sem.at[k], along_a(-k))

    for k in order:
        got3[k].wait_recv()
    stats = [r2[k, HD : HD + 16, :].astype(F32) for k in range(n)]
    tops = [s[0:1] + s[1:2] for s in stats]
    top = functools.reduce(jnp.maximum, tops)
    numer = jnp.zeros((HD, lanes), F32)
    denom = jnp.zeros((1, lanes), F32)
    for k in range(n):
        factor = jnp.exp(tops[k] - top)
        denom = denom + (stats[k][2:3] + stats[k][3:4]) * factor
        numer = numer + r2[k, 0:HD, :].astype(F32) * factor

    first = iota((HD, lanes), 1) < rows

    def turn(x):
        x = jnp.concatenate([jnp.where(first, x, 0.0), jnp.where(first, 0.0, x)], axis=0).T
        return x[0:rows] + x[rows : 2 * rows]

    numer = turn(numer)
    both = turn(jnp.where(iota((HD, lanes), 0) < HD // 2, top, denom))
    for k in range(n):
        target = r3s.at[k] if k else r3.at[0]
        target[0:8, :] = numer[8 * k : 8 * k + 8]
        target[8:16, :] = both[8 * k : 8 * k + 8]
    got4 = {k: send(r3s.at[k], r3.at[k], r3s_sem.at[k], r3r_sem.at[k], along_b(-k)) for k in order}
    loads[12].wait()
    for k in order:
        got4[k].wait_recv()
    near = lax.rem(lane8, HD) < HD // 2
    tops, denoms = [], []
    for k in range(n):
        both = r3[k, 8:16, :]
        tops.append(jnp.where(near, both, pltpu.roll(both, HD // 2, 1)))
        denoms.append(jnp.where(near, pltpu.roll(both, W - HD // 2, 1), both))
    top = functools.reduce(jnp.maximum, tops, own)
    own_weight = jnp.exp(own - top)
    denom = own_weight
    numer = own_weight.astype(BF16).astype(F32) * v8
    for k in range(n):
        factor = jnp.exp(tops[k] - top)
        denom = denom + denoms[k] * factor
        numer = numer + r3[k, 0:8, :] * factor
    attended = (numer / denom).astype(BF16).astype(F32)
    attended = jnp.concatenate([jnp.where(upper, attended, 0.0), jnp.where(upper, 0.0, attended)], axis=1)
    part = dot(attended.astype(BF16), wo[...])
    part = part + pltpu.roll(part, RD, 0)
    for k in range(heads_n):
        xs[k] = tile_of(part[:, 2 * W * k : 2 * W * (k + 1)])
    got5 = [
        send(xs.at[(hd + k) % heads_n], xr.at[k], xs_sem.at[k], xr_sem.at[k], along_x(k)) for k in range(1, heads_n)
    ]
    summed = xs[hd]
    for k in range(1, heads_n):
        got5[k - 1].wait_recv()
        summed = summed + xr[k]
    summed = (summed + res[hd]).astype(BF16)
    out[:, 0:W] = summed[0:RD]
    out[:, W : 2 * W] = summed[RD : 2 * RD]
    for copy in sends:
        copy.wait_send()


def shards(
    hidden_in,
    norm_gain,
    w_query,
    w_key,
    w_value,
    w_out,
    cache_keys,
    cache_values,
    block_node,
    block_len,
    live_count,
    node_parent,
    request_leaf,
):
    side = math.isqrt(lax.axis_size("blk") // 2)
    heads_n = lax.axis_size("head")
    d_model = hidden_in.shape[1]
    cols = w_query.shape[1]
    n = side
    rows = n * 2 * RD
    lanes = 2 * rows
    nodes = -(-node_parent.shape[0] // W) * W
    vmem = pl.BlockSpec(memory_space=pltpu.VMEM)
    hbm = pl.BlockSpec(memory_space=pltpu.HBM)
    shape = jax.ShapeDtypeStruct
    new = shape((RD, cols), BF16)
    dma = pltpu.SemaphoreType.DMA
    return pl.pallas_call(
        functools.partial(kernel, side, heads_n),
        out_shape=(new, new, new),
        in_specs=[hbm] * 13,
        out_specs=(vmem, vmem, vmem),
        scratch_shapes=[
            pltpu.VMEM((RD, d_model), BF16),
            pltpu.VMEM((1, d_model), F32),
            pltpu.VMEM((1, node_parent.shape[0]), jnp.int32),
            pltpu.VMEM((1, request_leaf.shape[0]), jnp.int32),
            pltpu.VMEM((1, SL), jnp.int32),
            pltpu.VMEM((1, SL), jnp.int32),
            pltpu.VMEM((1, 1), jnp.int32),
            pltpu.VMEM((d_model, cols), BF16),
            pltpu.VMEM((d_model, cols), BF16),
            pltpu.VMEM((d_model, cols), BF16),
            pltpu.VMEM((cols, d_model), BF16),
            pltpu.VMEM((2 * SL, BT, cols), BF16),
            pltpu.VMEM((2 * SL, BT, cols), BF16),
            pltpu.VMEM((cols, 2 * SL * BT), BF16),
            pltpu.VMEM((2 * RD, d_model), F32),
            pltpu.VMEM((n, 2 * RD, W), F32),
            pltpu.VMEM((n, rows, W), BF16),
            pltpu.VMEM((8, W), F32),
            pltpu.VMEM((8, W), F32),
            pltpu.VMEM((1, nodes), F32),
            pltpu.VMEM((8, n * lanes), F32),
            pltpu.VMEM((n, HD + 16, lanes), BF16),
            pltpu.VMEM((n, HD + 16, lanes), BF16),
            pltpu.VMEM((n, 16, W), F32),
            pltpu.VMEM((n, 16, W), F32),
            pltpu.VMEM((heads_n, 8, W), F32),
            pltpu.VMEM((heads_n, 8, W), F32),
            pltpu.VMEM((heads_n, 8, W), F32),
            dma((13,)),
            dma((3,)),
            dma((3,)),
        ]
        + [dma((n,))] * 8
        + [dma((heads_n,))] * 2,
        compiler_params=pltpu.CompilerParams(
            collective_id=0, has_side_effects=True, vmem_limit_bytes=60 * 1024 * 1024
        ),
    )(
        hidden_in,
        norm_gain.reshape(1, -1),
        node_parent.reshape(1, -1),
        request_leaf.reshape(1, -1),
        block_node.reshape(1, -1),
        block_len.reshape(1, -1),
        live_count.reshape(1, -1),
        w_query,
        w_key,
        w_value,
        w_out,
        cache_keys,
        cache_values,
    )


def solution(mesh):
    in_specs = (
        P("blk", None),
        P(),
        P(None, "head"),
        P(None, "head"),
        P(None, "head"),
        P("head", None),
        P("blk", None, "head"),
        P("blk", None, "head"),
        P("blk"),
        P("blk"),
        P("blk"),
        P(),
        P(),
    )
    out_specs = (P("blk", "head"), P("blk", "head"), P("blk", "head"))
    return jax.shard_map(shards, mesh=mesh, in_specs=in_specs, out_specs=out_specs, check_vma=False)
```

```python
import functools
import math

import jax
import jax.numpy as jnp
from jax import lax
from jax.experimental import pallas as pl
from jax.experimental.pallas import tpu as pltpu
from jax.sharding import PartitionSpec as P

HD = 64
RD = 4
BT = 128
SL = 2
W = 128
MESH = pl.DeviceIdType.MESH
F32 = jnp.float32
BF16 = jnp.bfloat16

very_low = -1e30
low_top = -1e29
BATCHES8 = ((0, 1, 7), (2, 6), (3, 5, 4))


def iota(shape, axis):
    return lax.broadcasted_iota(jnp.int32, shape, axis)


def dot_nt(a, b):
    return lax.dot_general(a, b, (((1,), (1,)), ((), ())), preferred_element_type=F32)


def dot(a, b):
    return jnp.dot(a, b, preferred_element_type=F32)


def kernel(
    side,
    heads_n,
    hidden_h,
    gain_h,
    parent_h,
    leaf_h,
    node_h,
    len_h,
    live_h,
    wq_h,
    wk_h,
    wv_h,
    wo_h,
    ck_h,
    cv_h,
    outs,
    hidden,
    gain,
    parent,
    leaf,
    node,
    length,
    live,
    wq,
    wk,
    wv,
    wo,
    kbuf,
    vbuf,
    hid8,
    g1,
    g2,
    meta_send,
    meta_recv,
    par,
    pick,
    bias,
    back_s,
    back,
    xs,
    xr,
    res,
    lsem,
    csem,
    crem,
    g1s_sem,
    g1r_sem,
    g2s_sem,
    g2r_sem,
    bs_sem,
    br_sem,
    xs_sem,
    xr_sem,
):
    n = side
    rows = n * 2 * RD
    lanes = 2 * rows
    nodes = par.shape[1]
    total = leaf.shape[1]
    me = lax.axis_index("blk")
    hd = lax.axis_index("head")
    core = me % 2
    y = (me // 2) % n
    z = me // (2 * n)
    flip = 1 - core
    a = y * flip + z * core
    b = z * flip + y * core

    step_a = 2 * flip + 2 * n * core
    step_b = 2 * n * flip + 2 * core
    base_a = [(a + k) % n * step_a + core for k in range(n)]
    base_b = [(b + k) % n * step_b for k in range(n)]

    def plane(k, j):
        return {"blk": base_a[k % n] + base_b[j % n], "head": hd}

    def along_a(k):
        return plane(k, 0)

    def along_b(k):
        return plane(0, k)

    def along_x(k):
        return {"blk": me, "head": (hd + k) % heads_n}

    other = {"blk": me + 1 - 2 * core, "head": hd}

    barrier = pltpu.get_barrier_semaphore()
    for k in range(1, n):
        pl.semaphore_signal(barrier, inc=1, device_id=along_b(k), device_id_type=MESH)
    for k in range(1, n):
        pl.semaphore_signal(barrier, inc=1, device_id=along_a(k), device_id_type=MESH)
    pl.semaphore_signal(barrier, inc=1, device_id=other, device_id_type=MESH)
    for k in range(1, heads_n):
        pl.semaphore_signal(barrier, inc=1, device_id=along_x(k), device_id_type=MESH)

    loads = [
        pltpu.make_async_copy(src, dst, lsem.at[k])
        for k, (src, dst) in enumerate(
            [
                (hidden_h, hidden),
                (gain_h, gain),
                (wq_h, wq),
                (node_h, node),
                (len_h, length),
                (live_h, live),
                (wk_h, wk),
                (wv_h, wv),
                (cv_h, vbuf.at[pl.ds(0, SL)]),
                (ck_h, kbuf.at[pl.ds(0, SL)]),
                (parent_h, parent),
                (leaf_h, leaf),
                (wo_h, wo),
            ]
        )
    ]
    for load in loads:
        load.start()

    loads[0].wait()
    loads[1].wait()
    states = hidden[...].astype(F32)
    hid8[pl.ds(0, RD), :] = states
    hid8[pl.ds(RD, RD), :] = states
    h8 = hid8[...]
    inv = lax.rsqrt(jnp.mean(h8 * h8, axis=1, keepdims=True) + 1e-06)
    normed = (h8 * inv * gain[...]).astype(BF16)
    row8 = iota((2 * RD, W), 0)
    lane8 = iota((2 * RD, W), 1)
    upper = row8 < RD

    def tile_of(wide):
        return jnp.where(upper, wide[:, 0:W], wide[:, W : 2 * W])

    loads[2].wait()
    q8 = tile_of(dot(normed, wq[...]).astype(BF16).astype(F32))
    g1[0] = q8

    for k in (3, 4, 5):
        loads[k].wait()
    own_len = [jnp.where(s < live[:, 0:1], length[:, s : s + 1], 0).astype(F32) for s in range(SL)]
    own_node = [node[:, s : s + 1].astype(F32) for s in range(SL)]

    def slot_tile(first):
        tile = jnp.zeros((8, W), F32)
        for s in range(SL):
            tile = jnp.where(row8 == first + s, own_node[s], tile)
            tile = jnp.where(row8 == 4 + first + s, own_len[s], tile)
        return tile

    meta_send[...] = slot_tile(SL)

    sends = []

    def send(src, dst, send_sem, recv_sem, target, alone=True):
        copy = pltpu.make_async_remote_copy(
            src_ref=src,
            dst_ref=dst,
            send_sem=send_sem,
            recv_sem=recv_sem,
            device_id=target,
            device_id_type=MESH,
        )
        copy.start()
        if alone:
            sends.append(copy)
        return copy

    pl.semaphore_wait(barrier, 2 * (n - 1) + 1 + heads_n - 1)

    order = sorted(range(1, n), key=lambda k: -min(k, n - k))
    got1 = {k: send(g1.at[0], g1.at[k], g1s_sem.at[k], g1r_sem.at[k], along_b(k)) for k in order}
    got_meta = send(meta_send, meta_recv, csem.at[0], crem.at[0], other)
    got_v = send(cv_h, vbuf.at[pl.ds(SL, SL)], csem.at[1], crem.at[1], other)
    got_k = send(ck_h, kbuf.at[pl.ds(SL, SL)], csem.at[2], crem.at[2], other)

    loads[6].wait()
    k8 = dot(normed, wk[...]).astype(BF16)
    outs[1] = k8[0:RD, :]
    loads[7].wait()
    v8 = dot(normed, wv[...]).astype(BF16)
    outs[2] = v8[0:RD, :]
    k8 = tile_of(k8.astype(F32))
    v8 = tile_of(v8.astype(F32))
    prod = q8 * k8
    left = lane8 < HD
    own = jnp.where(
        left,
        jnp.sum(jnp.where(left, prod, 0.0), axis=1, keepdims=True),
        jnp.sum(jnp.where(left, 0.0, prod), axis=1, keepdims=True),
    )
    for k in range(heads_n):
        res[k] = tile_of(h8[:, 2 * W * k : 2 * W * (k + 1)])

    spot = iota((n * rows, 1), 0)
    at_i = lax.rem(a + n - spot // rows, n)
    at_j = lax.rem(b + n - lax.rem(spot // (2 * RD), n), n)
    at_z = at_j * flip + at_i * core
    at_y = at_i * flip + at_j * core
    request = ((at_z * n + at_y) * 2 + core) * RD + lax.rem(spot, RD)
    pick[...] = jnp.where(iota((1, total), 1) == request, 1.0, 0.0).astype(BF16)

    for k in range(1, n):
        got1[k].wait_recv()
    g2[0] = g1[...].reshape(rows, W).astype(BF16)
    got2 = {k: send(g2.at[0], g2.at[k], g2s_sem.at[k], g2r_sem.at[k], along_a(k)) for k in order}

    loads[10].wait()
    loads[11].wait()
    par[...] = jnp.full_like(par, -1.0)
    par[:, 0 : parent.shape[1]] = parent[...].astype(F32)
    node_of_row = iota((nodes, 1), 0).astype(F32)
    hop = jnp.where(node_of_row == par[...], 1.0, 0.0).astype(BF16)
    leaf_hot = jnp.where(node_of_row == leaf[...].astype(F32), 1.0, 0.0).astype(BF16)
    got_meta.wait_recv()
    slots = slot_tile(0) + meta_recv[...]
    slot_node = jnp.concatenate([slots] * (nodes // W), axis=1)
    slot_len = jnp.concatenate([pltpu.roll(slots, 4, 0)] * (nodes // W), axis=1)
    level = jnp.where(iota((8, nodes), 1).astype(F32) == slot_node, 1.0, 0.0)
    up1 = dot(level.astype(BF16), hop)
    up2 = dot(up1.astype(BF16), hop)
    seen = dot((level + up1 + up2).astype(BF16), leaf_hot)
    row_of = iota((8, total), 0)
    unseen = jnp.where(row_of < 2 * SL, 1.0 - seen, jnp.where(row_of == 2 * SL, 1.0, 0.0))
    unseen = jnp.concatenate([unseen, jnp.zeros((W - 8, total), F32)], axis=0).astype(BF16)
    unseen = dot_nt(pick[...], unseen).astype(BF16)
    spot1 = iota((1, BT), 1).astype(F32)
    ends = [jnp.where(spot1 < slots[4 + s : 5 + s, :], 0.0, very_low) for s in range(2 * SL)]
    ends = jnp.concatenate(ends, axis=1)
    tokens = 2 * SL * BT
    slot_row = iota((W, tokens), 0)
    hide = jnp.where(
        slot_row == 2 * SL,
        ends,
        jnp.where(slot_row == iota((W, tokens), 1) // BT, very_low, 0.0),
    ).astype(BF16)
    bias[...] = dot(unseen, hide).reshape(n, rows, tokens)

    loads[8].wait()
    got_v.wait_recv()
    values = vbuf[...].reshape(tokens, 2 * W)
    loads[9].wait()
    got_k.wait_recv()
    keys = kbuf[...].reshape(tokens, 2 * W)

    spread_row = iota((lanes, 2 * W), 0)
    spread_lane = iota((lanes, 2 * W), 1)
    spread = jnp.where(
        (spread_row // rows == lax.rem(spread_lane // HD, 2)) & (lax.rem(spread_row // RD, 2) == spread_lane // W),
        1.0,
        0.0,
    ).astype(BF16)
    low_half = lax.rem(iota((lanes, W), 0), 2 * RD) < RD
    lane = iota((rows, W), 1)
    first = lane < HD
    part_of = lax.rem(lane, HD) // 16

    def pair(x):
        return jnp.where(first, x[0:rows], x[rows : 2 * rows])

    def split(x):
        hi = x.astype(BF16).astype(F32)
        return hi, (x - hi).astype(BF16).astype(F32)

    def attend(batch):
        queries, hidden_bias = [], []
        for k in batch:
            block = g2[k]
            block = jnp.concatenate([block, block], axis=1)
            queries.append(jnp.concatenate([block, block], axis=0) * spread)
            hidden_bias += [bias[k], bias[k]]
        scores = dot_nt(jnp.concatenate(queries, axis=0), keys) + jnp.concatenate(hidden_bias, axis=0)
        top_hi, top_lo = split(jnp.maximum(jnp.max(scores, axis=1, keepdims=True), low_top))
        weights = jnp.exp(scores - (top_hi + top_lo))
        den_hi, den_lo = split(jnp.sum(weights, axis=1, keepdims=True))
        full = dot(weights.astype(BF16), values)
        for at, k in enumerate(batch):
            here = slice(at * lanes, (at + 1) * lanes)
            numer = pair(jnp.where(low_half, full[here, 0:W], full[here, W : 2 * W]))
            stats = jnp.where(
                part_of == 0,
                pair(top_hi[here]),
                jnp.where(part_of == 1, pair(top_lo[here]), jnp.where(part_of == 2, pair(den_hi[here]), pair(den_lo[here]))),
            )
            both = jnp.concatenate([numer.reshape(n, 8, W), stats.reshape(n, 8, W)], axis=1).astype(BF16)
            if k:
                back_s[n * k : n * (k + 1)] = both
            else:
                back_s[1:n] = both[1:n]
                back[0] = both[0]

    returned = None
    reach = [min(k, n - k) for k in range(n)]
    batches = BATCHES8 if n == 8 else (tuple(range(n)),)
    for batch in batches:
        for k in batch:
            if k:
                got2[k].wait_recv()
        attend(batch)
        pairs = [(k, j) for k in batch for j in range(n) if k or j]
        for k, j in sorted(pairs, key=lambda p: -reach[p[0]] - reach[p[1]]):
            slot = n * k + j
            send(back_s.at[slot], back.at[slot], bs_sem, br_sem, plane(-k, -j), False)
    others = pl.ds(1, n * n - 1)
    all_back = pltpu.make_async_copy(back_s.at[others], back.at[others], br_sem)
    loads[12].wait()
    all_back.wait()
    pieces = back[...].astype(F32).reshape(n * n, 2, 8, W)
    numers = pieces[:, 0].reshape(n * n * 8, W)
    stats = pieces[:, 1].reshape(n * n * 8, W)
    stats = stats + pltpu.roll(stats, W - 16, 1)
    top = jnp.maximum(jnp.max(stats.reshape(n * n, 8, W), axis=0), own)
    lead = lax.rem(lane8, HD) < 16
    top = jnp.where(lead, top, 0.0)
    factor = jnp.where(lead[None], jnp.exp(stats.reshape(n * n, 8, W) - top[None]), 0.0).reshape(n * n * 8, W)
    factor = factor + pltpu.roll(factor, 16, 1)
    factor = factor + pltpu.roll(factor, 32, 1)
    numer = jnp.sum((numers * factor).reshape(n * n, 8, W), axis=0)
    denom = jnp.sum((stats * factor).reshape(n * n, 8, W), axis=0)
    top = top + pltpu.roll(top, 16, 1)
    top = top + pltpu.roll(top, 32, 1)
    denom = jnp.where((lax.rem(lane8, HD) >= 32) & (lax.rem(lane8, HD) < 48), denom, 0.0)
    denom = denom + pltpu.roll(denom, 16, 1)
    denom = denom + pltpu.roll(denom, W - 32, 1)
    own_weight = jnp.exp(own - top)
    denom = denom + own_weight
    numer = numer + own_weight.astype(BF16).astype(F32) * v8
    attended = (numer / denom).astype(BF16).astype(F32)
    attended = jnp.concatenate([jnp.where(upper, attended, 0.0), jnp.where(upper, 0.0, attended)], axis=1)
    part = dot(attended.astype(BF16), wo[...])
    part = part + pltpu.roll(part, RD, 0)
    for k in range(heads_n):
        xs[k] = tile_of(part[:, 2 * W * k : 2 * W * (k + 1)])
    got5 = [
        send(xs.at[(hd + k) % heads_n], xr.at[k], xs_sem.at[k], xr_sem.at[k], along_x(k)) for k in range(1, heads_n)
    ]
    summed = xs[hd]
    for k in range(1, heads_n):
        got5[k - 1].wait_recv()
        summed = summed + xr[k]
    summed = (summed + res[hd]).astype(BF16)
    outs[0, :, 0:W] = summed[0:RD]
    outs[0, :, W : 2 * W] = summed[RD : 2 * RD]
    for copy in sends:
        copy.wait_send()
    pltpu.make_async_copy(back_s.at[others], back.at[others], bs_sem).wait()


def shards(
    hidden_in,
    norm_gain,
    w_query,
    w_key,
    w_value,
    w_out,
    cache_keys,
    cache_values,
    block_node,
    block_len,
    live_count,
    node_parent,
    request_leaf,
):
    side = math.isqrt(lax.axis_size("blk") // 2)
    heads_n = lax.axis_size("head")
    d_model = hidden_in.shape[1]
    cols = w_query.shape[1]
    n = side
    rows = n * 2 * RD
    lanes = 2 * rows
    nodes = -(-node_parent.shape[0] // W) * W
    vmem = pl.BlockSpec(memory_space=pltpu.VMEM)
    hbm = pl.BlockSpec(memory_space=pltpu.HBM)
    shape = jax.ShapeDtypeStruct
    new = shape((3, RD, cols), BF16)
    dma = pltpu.SemaphoreType.DMA
    packed = pl.pallas_call(
        functools.partial(kernel, side, heads_n),
        out_shape=new,
        in_specs=[hbm] * 13,
        out_specs=vmem,
        scratch_shapes=[
            pltpu.VMEM((RD, d_model), BF16),
            pltpu.VMEM((1, d_model), F32),
            pltpu.VMEM((1, node_parent.shape[0]), jnp.int32),
            pltpu.VMEM((1, request_leaf.shape[0]), jnp.int32),
            pltpu.VMEM((1, SL), jnp.int32),
            pltpu.VMEM((1, SL), jnp.int32),
            pltpu.VMEM((1, 1), jnp.int32),
            pltpu.VMEM((d_model, cols), BF16),
            pltpu.VMEM((d_model, cols), BF16),
            pltpu.VMEM((d_model, cols), BF16),
            pltpu.VMEM((cols, d_model), BF16),
            pltpu.VMEM((2 * SL, BT, cols), BF16),
            pltpu.VMEM((2 * SL, BT, cols), BF16),
            pltpu.VMEM((2 * RD, d_model), F32),
            pltpu.VMEM((n, 2 * RD, W), F32),
            pltpu.VMEM((n, rows, W), BF16),
            pltpu.VMEM((8, W), F32),
            pltpu.VMEM((8, W), F32),
            pltpu.VMEM((1, nodes), F32),
            pltpu.VMEM((n * rows, request_leaf.shape[0]), BF16),
            pltpu.VMEM((n, rows, 2 * SL * BT), F32),
            pltpu.VMEM((n * n, 16, W), BF16),
            pltpu.VMEM((n * n, 16, W), BF16),
            pltpu.VMEM((heads_n, 8, W), F32),
            pltpu.VMEM((heads_n, 8, W), F32),
            pltpu.VMEM((heads_n, 8, W), F32),
            dma((13,)),
            dma((3,)),
            dma((3,)),
        ]
        + [dma((n,))] * 4
        + [dma(()), dma(())]
        + [dma((heads_n,))] * 2,
        compiler_params=pltpu.CompilerParams(
            collective_id=0, has_side_effects=True, vmem_limit_bytes=60 * 1024 * 1024
        ),
    )(
        hidden_in,
        norm_gain.reshape(1, -1),
        node_parent.reshape(1, -1),
        request_leaf.reshape(1, -1),
        block_node.reshape(1, -1),
        block_len.reshape(1, -1),
        live_count.reshape(1, -1),
        w_query,
        w_key,
        w_value,
        w_out,
        cache_keys,
        cache_values,
    )
    return packed[0], packed[1], packed[2]


def solution(mesh):
    in_specs = (
        P("blk", None),
        P(),
        P(None, "head"),
        P(None, "head"),
        P(None, "head"),
        P("head", None),
        P("blk", None, "head"),
        P("blk", None, "head"),
        P("blk"),
        P("blk"),
        P("blk"),
        P(),
        P(),
    )
    out_specs = (P("blk", "head"), P("blk", "head"), P("blk", "head"))
    return jax.shard_map(shards, mesh=mesh, in_specs=in_specs, out_specs=out_specs, check_vma=False)
```

```python
import functools
import math

import jax
import jax.numpy as jnp
from jax import lax
from jax.experimental import pallas as pl
from jax.experimental.pallas import tpu as pltpu
from jax.sharding import PartitionSpec as P

HD = 64
RD = 4
BT = 128
SL = 2
W = 128
MESH = pl.DeviceIdType.MESH
F32 = jnp.float32
BF16 = jnp.bfloat16

very_low = -1e30
low_top = -1e29
BATCHES8 = ((0, 1, 7), (2, 6), (3, 5, 4))


def iota(shape, axis):
    return lax.broadcasted_iota(jnp.int32, shape, axis)


def dot_nt(a, b):
    return lax.dot_general(a, b, (((1,), (1,)), ((), ())), preferred_element_type=F32)


def dot(a, b):
    return jnp.dot(a, b, preferred_element_type=F32)


def kernel(
    side,
    heads_n,
    live,
    hidden_h,
    gain_h,
    parent_h,
    leaf_h,
    node_h,
    len_h,
    wq_h,
    wk_h,
    wv_h,
    wo_h,
    ck_h,
    cv_h,
    outs,
    hidden,
    gain,
    parent,
    leaf,
    node,
    length,
    wq,
    wk,
    wv,
    wo,
    kbuf,
    vbuf,
    hid8,
    g1,
    g2,
    meta_send,
    meta_recv,
    par,
    pick,
    bias,
    back_s,
    back,
    xs,
    xr,
    res,
    lsem,
    csem,
    crem,
    g1s_sem,
    g1r_sem,
    g2s_sem,
    g2r_sem,
    bs_sem,
    br_sem,
    xs_sem,
    xr_sem,
):
    n = side
    rows = n * 2 * RD
    lanes = 2 * rows
    nodes = par.shape[1]
    total = leaf.shape[1]
    me = lax.axis_index("blk")
    hd = lax.axis_index("head")
    core = me % 2
    y = (me // 2) % n
    z = me // (2 * n)
    flip = 1 - core
    a = y * flip + z * core
    b = z * flip + y * core

    step_a = 2 * flip + 2 * n * core
    step_b = 2 * n * flip + 2 * core
    base_a = [(a + k) % n * step_a + core for k in range(n)]
    base_b = [(b + k) % n * step_b for k in range(n)]

    def plane(k, j):
        return {"blk": base_a[k % n] + base_b[j % n], "head": hd}

    def along_a(k):
        return plane(k, 0)

    def along_b(k):
        return plane(0, k)

    def along_x(k):
        return {"blk": me, "head": (hd + k) % heads_n}

    other = {"blk": me + 1 - 2 * core, "head": hd}

    order = sorted(range(1, n), key=lambda k: -min(k, n - k))
    xorder = sorted(range(1, heads_n), key=lambda k: -min(k, heads_n - k))
    loads = [
        pltpu.make_async_copy(src, dst, lsem.at[k])
        for k, (src, dst) in enumerate(
            [
                (hidden_h, hidden),
                (gain_h, gain),
                (wq_h, wq),
                (node_h, node),
                (len_h, length),
                (wk_h, wk),
                (wv_h, wv),
                (cv_h, vbuf.at[pl.ds(0, SL)]),
                (ck_h, kbuf.at[pl.ds(0, SL)]),
                (parent_h, parent),
                (leaf_h, leaf),
                (wo_h, wo),
            ]
        )
    ]
    for load in loads[:3]:
        load.start()

    barrier = pltpu.get_barrier_semaphore()
    for k in order:
        pl.semaphore_signal(barrier, inc=1, device_id=along_b(k), device_id_type=MESH)
    for k in order:
        pl.semaphore_signal(barrier, inc=1, device_id=along_a(k), device_id_type=MESH)
    pl.semaphore_signal(barrier, inc=1, device_id=other, device_id_type=MESH)
    for k in xorder:
        pl.semaphore_signal(barrier, inc=1, device_id=along_x(k), device_id_type=MESH)
    for load in loads[3:]:
        load.start()

    loads[0].wait()
    loads[1].wait()
    states = hidden[...].astype(F32)
    hid8[pl.ds(0, RD), :] = states
    hid8[pl.ds(RD, RD), :] = states
    h8 = hid8[...]
    inv = lax.rsqrt(jnp.mean(h8 * h8, axis=1, keepdims=True) + 1e-06)
    normed = (h8 * inv * gain[...]).astype(BF16)
    row8 = iota((2 * RD, W), 0)
    lane8 = iota((2 * RD, W), 1)
    upper = row8 < RD

    def tile_of(wide):
        return jnp.where(upper, wide[:, 0:W], wide[:, W : 2 * W])

    loads[2].wait()
    q8 = tile_of(dot(normed, wq[...]).astype(BF16).astype(F32))
    g1[0] = q8

    for k in (3, 4):
        loads[k].wait()
    own_len = [jnp.where(s < live[0], length[:, s : s + 1], 0).astype(F32) for s in range(SL)]
    own_node = [node[:, s : s + 1].astype(F32) for s in range(SL)]

    def slot_tile(first):
        tile = jnp.zeros((8, W), F32)
        for s in range(SL):
            tile = jnp.where(row8 == first + s, own_node[s], tile)
            tile = jnp.where(row8 == 4 + first + s, own_len[s], tile)
        return tile

    meta_send[...] = slot_tile(SL)

    sends = []

    def send(src, dst, send_sem, recv_sem, target, alone=True):
        copy = pltpu.make_async_remote_copy(
            src_ref=src,
            dst_ref=dst,
            send_sem=send_sem,
            recv_sem=recv_sem,
            device_id=target,
            device_id_type=MESH,
        )
        copy.start()
        if alone:
            sends.append(copy)
        return copy

    pl.semaphore_wait(barrier, 2 * (n - 1) + 1 + heads_n - 1)

    got1 = {k: send(g1.at[0], g1.at[k], g1s_sem.at[k], g1r_sem.at[k], along_b(k)) for k in order}
    got_meta = send(meta_send, meta_recv, csem.at[0], crem.at[0], other)
    got_v = send(cv_h, vbuf.at[pl.ds(SL, SL)], csem.at[1], crem.at[1], other)
    got_k = send(ck_h, kbuf.at[pl.ds(SL, SL)], csem.at[2], crem.at[2], other)

    loads[5].wait()
    k8 = dot(normed, wk[...]).astype(BF16)
    outs[1] = k8[0:RD, :]
    loads[6].wait()
    v8 = dot(normed, wv[...]).astype(BF16)
    outs[2] = v8[0:RD, :]
    k8 = tile_of(k8.astype(F32))
    v8 = tile_of(v8.astype(F32))
    prod = q8 * k8
    left = lane8 < HD
    own = jnp.where(
        left,
        jnp.sum(jnp.where(left, prod, 0.0), axis=1, keepdims=True),
        jnp.sum(jnp.where(left, 0.0, prod), axis=1, keepdims=True),
    )
    for k in range(heads_n):
        res[k] = tile_of(h8[:, 2 * W * k : 2 * W * (k + 1)])

    spot = iota((n * rows, 1), 0)
    at_i = lax.rem(a + n - spot // rows, n)
    at_j = lax.rem(b + n - lax.rem(spot // (2 * RD), n), n)
    at_z = at_j * flip + at_i * core
    at_y = at_i * flip + at_j * core
    request = ((at_z * n + at_y) * 2 + core) * RD + lax.rem(spot, RD)
    pick[...] = jnp.where(iota((1, total), 1) == request, 1.0, 0.0).astype(BF16)

    for k in range(1, n):
        got1[k].wait_recv()
    g2[0] = g1[...].reshape(rows, W).astype(BF16)
    got2 = {k: send(g2.at[0], g2.at[k], g2s_sem.at[k], g2r_sem.at[k], along_a(k)) for k in order}

    loads[9].wait()
    loads[10].wait()
    par[...] = jnp.full_like(par, -1.0)
    par[:, 0 : parent.shape[1]] = parent[...].astype(F32)
    node_of_row = iota((nodes, 1), 0).astype(F32)
    hop = jnp.where(node_of_row == par[...], 1.0, 0.0).astype(BF16)
    leaf_hot = jnp.where(node_of_row == leaf[...].astype(F32), 1.0, 0.0).astype(BF16)
    got_meta.wait_recv()
    slots = slot_tile(0) + meta_recv[...]
    slot_node = jnp.concatenate([slots] * (nodes // W), axis=1)
    slot_len = jnp.concatenate([pltpu.roll(slots, 4, 0)] * (nodes // W), axis=1)
    level = jnp.where(iota((8, nodes), 1).astype(F32) == slot_node, 1.0, 0.0)
    up1 = dot(level.astype(BF16), hop)
    up2 = dot(up1.astype(BF16), hop)
    seen = dot((level + up1 + up2).astype(BF16), leaf_hot)
    row_of = iota((8, total), 0)
    unseen = jnp.where(row_of < 2 * SL, 1.0 - seen, jnp.where(row_of == 2 * SL, 1.0, 0.0))
    unseen = jnp.concatenate([unseen, jnp.zeros((W - 8, total), F32)], axis=0).astype(BF16)
    unseen = dot_nt(pick[...], unseen).astype(BF16)
    spot1 = iota((1, BT), 1).astype(F32)
    ends = [jnp.where(spot1 < slots[4 + s : 5 + s, :], 0.0, very_low) for s in range(2 * SL)]
    ends = jnp.concatenate(ends, axis=1)
    tokens = 2 * SL * BT
    slot_row = iota((W, tokens), 0)
    hide = jnp.where(
        slot_row == 2 * SL,
        ends,
        jnp.where(slot_row == iota((W, tokens), 1) // BT, very_low, 0.0),
    ).astype(BF16)
    bias[...] = dot(unseen, hide).reshape(n, rows, tokens)

    loads[7].wait()
    got_v.wait_recv()
    values = vbuf[...].reshape(tokens, 2 * W)
    loads[8].wait()
    got_k.wait_recv()
    keys = kbuf[...].reshape(tokens, 2 * W)

    spread_row = iota((lanes, 2 * W), 0)
    spread_lane = iota((lanes, 2 * W), 1)
    spread = jnp.where(
        (spread_row // rows == lax.rem(spread_lane // HD, 2)) & (lax.rem(spread_row // RD, 2) == spread_lane // W),
        1.0,
        0.0,
    ).astype(BF16)
    low_half = lax.rem(iota((lanes, W), 0), 2 * RD) < RD
    lane = iota((rows, W), 1)
    first = lane < HD
    part_of = lax.rem(lane, HD) // 16

    def pair(x):
        return jnp.where(first, x[0:rows], x[rows : 2 * rows])

    def split(x):
        hi = x.astype(BF16).astype(F32)
        return hi, (x - hi).astype(BF16).astype(F32)

    def attend(batch):
        queries, hidden_bias = [], []
        for k in batch:
            block = g2[k]
            block = jnp.concatenate([block, block], axis=1)
            queries.append(jnp.concatenate([block, block], axis=0) * spread)
            hidden_bias += [bias[k], bias[k]]
        scores = dot_nt(jnp.concatenate(queries, axis=0), keys) + jnp.concatenate(hidden_bias, axis=0)
        top_hi, top_lo = split(jnp.maximum(jnp.max(scores, axis=1, keepdims=True), low_top))
        weights = jnp.exp(scores - (top_hi + top_lo))
        den_hi, den_lo = split(jnp.sum(weights, axis=1, keepdims=True))
        full = dot(weights.astype(BF16), values)
        for at, k in enumerate(batch):
            here = slice(at * lanes, (at + 1) * lanes)
            numer = pair(jnp.where(low_half, full[here, 0:W], full[here, W : 2 * W]))
            stats = jnp.where(
                part_of == 0,
                pair(top_hi[here]),
                jnp.where(part_of == 1, pair(top_lo[here]), jnp.where(part_of == 2, pair(den_hi[here]), pair(den_lo[here]))),
            )
            both = jnp.concatenate([numer.reshape(n, 8, W), stats.reshape(n, 8, W)], axis=1).astype(BF16)
            if k:
                back_s[n * k : n * (k + 1)] = both
            else:
                back_s[1:n] = both[1:n]
                back[0] = both[0]

    returned = None
    reach = [min(k, n - k) for k in range(n)]
    batches = BATCHES8 if n == 8 else (tuple(range(n)),)
    for batch in batches:
        for k in batch:
            if k:
                got2[k].wait_recv()
        attend(batch)
        pairs = [(k, j) for k in batch for j in range(n) if k or j]
        for k, j in sorted(pairs, key=lambda p: -reach[p[0]] - reach[p[1]]):
            slot = n * k + j
            send(back_s.at[slot], back.at[slot], bs_sem, br_sem, plane(-k, -j), False)
    others = pl.ds(1, n * n - 1)
    all_back = pltpu.make_async_copy(back_s.at[others], back.at[others], br_sem)
    loads[11].wait()
    all_back.wait()
    pieces = back[...].astype(F32).reshape(n * n, 2, 8, W)
    numers = pieces[:, 0].reshape(n * n * 8, W)
    stats = pieces[:, 1].reshape(n * n * 8, W)
    stats = stats + pltpu.roll(stats, W - 16, 1)
    top = jnp.maximum(jnp.max(stats.reshape(n * n, 8, W), axis=0), own)
    lead = lax.rem(lane8, HD) < 16
    top = jnp.where(lead, top, 0.0)
    factor = jnp.where(lead[None], jnp.exp(stats.reshape(n * n, 8, W) - top[None]), 0.0).reshape(n * n * 8, W)
    factor = factor + pltpu.roll(factor, 16, 1)
    factor = factor + pltpu.roll(factor, 32, 1)
    numer = jnp.sum((numers * factor).reshape(n * n, 8, W), axis=0)
    denom = jnp.sum((stats * factor).reshape(n * n, 8, W), axis=0)
    top = top + pltpu.roll(top, 16, 1)
    top = top + pltpu.roll(top, 32, 1)
    denom = jnp.where((lax.rem(lane8, HD) >= 32) & (lax.rem(lane8, HD) < 48), denom, 0.0)
    denom = denom + pltpu.roll(denom, 16, 1)
    denom = denom + pltpu.roll(denom, W - 32, 1)
    own_weight = jnp.exp(own - top)
    denom = denom + own_weight
    numer = numer + own_weight.astype(BF16).astype(F32) * v8
    attended = (numer / denom).astype(BF16).astype(F32)
    attended = jnp.concatenate([jnp.where(upper, attended, 0.0), jnp.where(upper, 0.0, attended)], axis=1)
    part = dot(attended.astype(BF16), wo[...])
    part = part + pltpu.roll(part, RD, 0)
    for k in range(heads_n):
        xs[k] = tile_of(part[:, 2 * W * k : 2 * W * (k + 1)])
    got5 = {
        k: send(xs.at[(hd + k) % heads_n], xr.at[k], xs_sem.at[k], xr_sem.at[k], along_x(k)) for k in xorder
    }
    summed = xs[hd]
    for k in range(1, heads_n):
        got5[k].wait_recv()
        summed = summed + xr[k]
    summed = (summed + res[hd]).astype(BF16)
    outs[0, :, 0:W] = summed[0:RD]
    outs[0, :, W : 2 * W] = summed[RD : 2 * RD]
    for copy in sends:
        copy.wait_send()
    pltpu.make_async_copy(back_s.at[others], back.at[others], bs_sem).wait()


def shards(
    hidden_in,
    norm_gain,
    w_query,
    w_key,
    w_value,
    w_out,
    cache_keys,
    cache_values,
    block_node,
    block_len,
    live_count,
    node_parent,
    request_leaf,
):
    side = math.isqrt(lax.axis_size("blk") // 2)
    heads_n = lax.axis_size("head")
    d_model = hidden_in.shape[1]
    cols = w_query.shape[1]
    n = side
    rows = n * 2 * RD
    lanes = 2 * rows
    nodes = -(-node_parent.shape[0] // W) * W
    vmem = pl.BlockSpec(memory_space=pltpu.VMEM)
    hbm = pl.BlockSpec(memory_space=pltpu.HBM)
    shape = jax.ShapeDtypeStruct
    new = shape((3, RD, cols), BF16)
    dma = pltpu.SemaphoreType.DMA
    packed = pl.pallas_call(
        functools.partial(kernel, side, heads_n),
        out_shape=new,
        in_specs=[pl.BlockSpec(memory_space=pltpu.SMEM)] + [hbm] * 12,
        out_specs=vmem,
        scratch_shapes=[
            pltpu.VMEM((RD, d_model), BF16),
            pltpu.VMEM((1, d_model), F32),
            pltpu.VMEM((1, node_parent.shape[0]), jnp.int32),
            pltpu.VMEM((1, request_leaf.shape[0]), jnp.int32),
            pltpu.VMEM((1, SL), jnp.int32),
            pltpu.VMEM((1, SL), jnp.int32),
            pltpu.VMEM((d_model, cols), BF16),
            pltpu.VMEM((d_model, cols), BF16),
            pltpu.VMEM((d_model, cols), BF16),
            pltpu.VMEM((cols, d_model), BF16),
            pltpu.VMEM((2 * SL, BT, cols), BF16),
            pltpu.VMEM((2 * SL, BT, cols), BF16),
            pltpu.VMEM((2 * RD, d_model), F32),
            pltpu.VMEM((n, 2 * RD, W), F32),
            pltpu.VMEM((n, rows, W), BF16),
            pltpu.VMEM((8, W), F32),
            pltpu.VMEM((8, W), F32),
            pltpu.VMEM((1, nodes), F32),
            pltpu.VMEM((n * rows, request_leaf.shape[0]), BF16),
            pltpu.VMEM((n, rows, 2 * SL * BT), F32),
            pltpu.VMEM((n * n, 16, W), BF16),
            pltpu.VMEM((n * n, 16, W), BF16),
            pltpu.VMEM((heads_n, 8, W), F32),
            pltpu.VMEM((heads_n, 8, W), F32),
            pltpu.VMEM((heads_n, 8, W), F32),
            dma((12,)),
            dma((3,)),
            dma((3,)),
        ]
        + [dma((n,))] * 4
        + [dma(()), dma(())]
        + [dma((heads_n,))] * 2,
        compiler_params=pltpu.CompilerParams(
            collective_id=0, has_side_effects=True, vmem_limit_bytes=48 * 1024 * 1024
        ),
    )(
        live_count,
        *(
            pltpu.with_memory_space_constraint(x, pltpu.HBM)
            for x in (
                hidden_in,
                norm_gain.reshape(1, -1),
                node_parent.reshape(1, -1),
                request_leaf.reshape(1, -1),
                block_node.reshape(1, -1),
                block_len.reshape(1, -1),
                w_query,
                w_key,
                w_value,
                w_out,
                cache_keys,
                cache_values,
            )
        )
    )

    return packed[0], packed[1], packed[2]


def solution(mesh):
    in_specs = (
        P("blk", None),
        P(),
        P(None, "head"),
        P(None, "head"),
        P(None, "head"),
        P("head", None),
        P("blk", None, "head"),
        P("blk", None, "head"),
        P("blk"),
        P("blk"),
        P("blk"),
        P(),
        P(),
    )
    out_specs = (P("blk", "head"), P("blk", "head"), P("blk", "head"))
    return jax.shard_map(shards, mesh=mesh, in_specs=in_specs, out_specs=out_specs, check_vma=False)
```

```python
import functools
import math

import jax
import jax.numpy as jnp
from jax import lax
from jax.experimental import pallas as pl
from jax.experimental.pallas import tpu as pltpu
from jax.sharding import PartitionSpec as P

HD = 64
RD = 4
BT = 128
SL = 2
W = 128
MESH = pl.DeviceIdType.MESH
F32 = jnp.float32
BF16 = jnp.bfloat16

very_low = -1e30
low_top = -1e29
BATCHES8 = ((0, 1, 7), (2, 6), (3, 5, 4))


def iota(shape, axis):
    return lax.broadcasted_iota(jnp.int32, shape, axis)


def dot_nt(a, b):
    return lax.dot_general(a, b, (((1,), (1,)), ((), ())), preferred_element_type=F32)


def dot(a, b):
    return jnp.dot(a, b, preferred_element_type=F32)


def kernel(
    side,
    heads_n,
    live,
    hidden_h,
    gain_h,
    parent_h,
    leaf_h,
    node_h,
    len_h,
    wq_h,
    wk_h,
    wv_h,
    wo_h,
    ck_h,
    cv_h,
    outs,
    hidden,
    gain,
    parent,
    leaf,
    node,
    length,
    wq,
    wk,
    wv,
    wo,
    kbuf,
    vbuf,
    hid8,
    g1,
    g2,
    meta_send,
    meta_recv,
    par,
    pick,
    bias,
    back_s,
    back,
    xs,
    xr,
    res,
    lsem,
    csem,
    crem,
    g1s_sem,
    g1r_sem,
    g2s_sem,
    g2r_sem,
    bs_sem,
    br_sem,
    xs_sem,
    xr_sem,
):
    n = side
    rows = n * 2 * RD
    lanes = 2 * rows
    nodes = par.shape[1]
    total = leaf.shape[1]
    me = lax.axis_index("blk")
    hd = lax.axis_index("head")
    core = me % 2
    y = (me // 2) % n
    z = me // (2 * n)
    flip = 1 - core
    a = y * flip + z * core
    b = z * flip + y * core

    step_a = 2 * flip + 2 * n * core
    step_b = 2 * n * flip + 2 * core
    base_a = [(a + k) % n * step_a + core for k in range(n)]
    base_b = [(b + k) % n * step_b for k in range(n)]

    def plane(k, j):
        return {"blk": base_a[k % n] + base_b[j % n], "head": hd}

    def along_a(k):
        return plane(k, 0)

    def along_b(k):
        return plane(0, k)

    def along_x(k):
        return {"blk": me, "head": (hd + k) % heads_n}

    other = {"blk": me + 1 - 2 * core, "head": hd}

    order = sorted(range(1, n), key=lambda k: -min(k, n - k))
    xorder = sorted(range(1, heads_n), key=lambda k: -min(k, heads_n - k))
    loads = [
        pltpu.make_async_copy(src, dst, lsem.at[k])
        for k, (src, dst) in enumerate(
            [
                (hidden_h, hidden),
                (gain_h, gain),
                (wq_h, wq),
                (node_h, node),
                (len_h, length),
                (wk_h, wk),
                (wv_h, wv),
                (cv_h, vbuf.at[pl.ds(0, SL)]),
                (ck_h, kbuf.at[pl.ds(0, SL)]),
                (parent_h, parent),
                (leaf_h, leaf),
                (wo_h, wo),
            ]
        )
    ]
    for load in loads[:3]:
        load.start()

    barrier = pltpu.get_barrier_semaphore()
    for k in order:
        pl.semaphore_signal(barrier, inc=1, device_id=along_b(k), device_id_type=MESH)
    for k in order:
        pl.semaphore_signal(barrier, inc=1, device_id=along_a(k), device_id_type=MESH)
    pl.semaphore_signal(barrier, inc=1, device_id=other, device_id_type=MESH)
    for k in xorder:
        pl.semaphore_signal(barrier, inc=1, device_id=along_x(k), device_id_type=MESH)
    for load in loads[3:]:
        load.start()

    loads[0].wait()
    loads[1].wait()
    states = hidden[...].astype(F32)
    hid8[pl.ds(0, RD), :] = states
    hid8[pl.ds(RD, RD), :] = states
    h8 = hid8[...]
    inv = lax.rsqrt(jnp.mean(h8 * h8, axis=1, keepdims=True) + 1e-06)
    normed = (h8 * inv * gain[...]).astype(BF16)
    row8 = iota((2 * RD, W), 0)
    lane8 = iota((2 * RD, W), 1)
    upper = row8 < RD

    def tile_of(wide):
        return jnp.where(upper, wide[:, 0:W], wide[:, W : 2 * W])

    loads[2].wait()
    q8 = tile_of(dot(normed, wq[...]).astype(BF16).astype(F32))
    g1[0] = q8

    for k in (3, 4):
        loads[k].wait()
    own_len = [jnp.where(s < live[0], length[:, s : s + 1], 0).astype(F32) for s in range(SL)]
    own_node = [node[:, s : s + 1].astype(F32) for s in range(SL)]

    def slot_tile(first):
        tile = jnp.zeros((8, W), F32)
        for s in range(SL):
            tile = jnp.where(row8 == first + s, own_node[s], tile)
            tile = jnp.where(row8 == 4 + first + s, own_len[s], tile)
        return tile

    meta_send[...] = slot_tile(SL)

    sends = []

    def send(src, dst, send_sem, recv_sem, target, alone=True):
        copy = pltpu.make_async_remote_copy(
            src_ref=src,
            dst_ref=dst,
            send_sem=send_sem,
            recv_sem=recv_sem,
            device_id=target,
            device_id_type=MESH,
        )
        copy.start()
        if alone:
            sends.append(copy)
        return copy

    pl.semaphore_wait(barrier, 2 * (n - 1) + 1 + heads_n - 1)

    got1 = {k: send(g1.at[0], g1.at[k], g1s_sem.at[k], g1r_sem.at[k], along_b(k)) for k in order}
    got_meta = send(meta_send, meta_recv, csem.at[0], crem.at[0], other)
    got_v = send(cv_h, vbuf.at[pl.ds(SL, SL)], csem.at[1], crem.at[1], other)
    got_k = send(ck_h, kbuf.at[pl.ds(SL, SL)], csem.at[2], crem.at[2], other)

    loads[5].wait()
    k8 = dot(normed, wk[...]).astype(BF16)
    outs[1] = k8[0:RD, :]
    loads[6].wait()
    v8 = dot(normed, wv[...]).astype(BF16)
    outs[2] = v8[0:RD, :]
    k8 = tile_of(k8.astype(F32))
    v8 = tile_of(v8.astype(F32))
    prod = q8 * k8
    left = lane8 < HD
    own = jnp.where(
        left,
        jnp.sum(jnp.where(left, prod, 0.0), axis=1, keepdims=True),
        jnp.sum(jnp.where(left, 0.0, prod), axis=1, keepdims=True),
    )
    for k in range(heads_n):
        res[k] = tile_of(h8[:, 2 * W * k : 2 * W * (k + 1)])

    spot = iota((n * rows, 1), 0)
    at_i = lax.rem(a + n - spot // rows, n)
    at_j = lax.rem(b + n - lax.rem(spot // (2 * RD), n), n)
    at_z = at_j * flip + at_i * core
    at_y = at_i * flip + at_j * core
    request = ((at_z * n + at_y) * 2 + core) * RD + lax.rem(spot, RD)
    pick[...] = jnp.where(iota((1, total), 1) == request, 1.0, 0.0).astype(BF16)

    for k in range(1, n):
        got1[k].wait_recv()
    g2[0] = g1[...].reshape(rows, W).astype(BF16)
    got2 = {k: send(g2.at[0], g2.at[k], g2s_sem.at[k], g2r_sem.at[k], along_a(k)) for k in order}

    loads[9].wait()
    loads[10].wait()
    par[...] = jnp.full_like(par, -1.0)
    par[:, 0 : parent.shape[1]] = parent[...].astype(F32)
    node_of_row = iota((nodes, 1), 0).astype(F32)
    hop = jnp.where(node_of_row == par[...], 1.0, 0.0).astype(BF16)
    leaf_hot = jnp.where(node_of_row == leaf[...].astype(F32), 1.0, 0.0).astype(BF16)
    got_meta.wait_recv()
    slots = slot_tile(0) + meta_recv[...]
    slot_node = jnp.concatenate([slots] * (nodes // W), axis=1)
    slot_len = jnp.concatenate([pltpu.roll(slots, 4, 0)] * (nodes // W), axis=1)
    level = jnp.where(iota((8, nodes), 1).astype(F32) == slot_node, 1.0, 0.0)
    up1 = dot(level.astype(BF16), hop)
    up2 = dot(up1.astype(BF16), hop)
    seen = dot((level + up1 + up2).astype(BF16), leaf_hot)
    row_of = iota((8, total), 0)
    unseen = jnp.where(row_of < 2 * SL, 1.0 - seen, jnp.where(row_of == 2 * SL, 1.0, 0.0))
    unseen = jnp.concatenate([unseen, jnp.zeros((W - 8, total), F32)], axis=0).astype(BF16)
    unseen = dot_nt(pick[...], unseen).astype(BF16)
    spot1 = iota((1, BT), 1).astype(F32)
    ends = [jnp.where(spot1 < slots[4 + s : 5 + s, :], 0.0, very_low) for s in range(2 * SL)]
    ends = jnp.concatenate(ends, axis=1)
    tokens = 2 * SL * BT
    slot_row = iota((W, tokens), 0)
    hide = jnp.where(
        slot_row == 2 * SL,
        ends,
        jnp.where(slot_row == iota((W, tokens), 1) // BT, very_low, 0.0),
    ).astype(BF16)
    bias[...] = dot(unseen, hide).reshape(n, rows, tokens)

    loads[7].wait()
    got_v.wait_recv()
    values = vbuf[...].reshape(tokens, 2 * W)
    loads[8].wait()
    got_k.wait_recv()
    keys = kbuf[...].reshape(tokens, 2 * W)

    spread_row = iota((lanes, 2 * W), 0)
    spread_lane = iota((lanes, 2 * W), 1)
    spread = jnp.where(
        (spread_row // rows == lax.rem(spread_lane // HD, 2)) & (lax.rem(spread_row // RD, 2) == spread_lane // W),
        1.0,
        0.0,
    ).astype(BF16)
    low_half = lax.rem(iota((lanes, W), 0), 2 * RD) < RD
    lane = iota((rows, W), 1)
    first = lane < HD
    part_of = lax.rem(lane, HD) // 16

    def pair(x):
        return jnp.where(first, x[0:rows], x[rows : 2 * rows])

    def split(x):
        hi = x.astype(BF16).astype(F32)
        return hi, (x - hi).astype(BF16).astype(F32)

    def attend(batch):
        queries, hidden_bias = [], []
        for k in batch:
            block = g2[k]
            block = jnp.concatenate([block, block], axis=1)
            queries.append(jnp.concatenate([block, block], axis=0) * spread)
            hidden_bias += [bias[k], bias[k]]
        scores = dot_nt(jnp.concatenate(queries, axis=0), keys) + jnp.concatenate(hidden_bias, axis=0)
        top_hi, top_lo = split(jnp.maximum(jnp.max(scores, axis=1, keepdims=True), low_top))
        weights = jnp.exp(scores - (top_hi + top_lo))
        den_hi, den_lo = split(jnp.sum(weights, axis=1, keepdims=True))
        full = dot(weights.astype(BF16), values)
        for at, k in enumerate(batch):
            here = slice(at * lanes, (at + 1) * lanes)
            numer = pair(jnp.where(low_half, full[here, 0:W], full[here, W : 2 * W]))
            stats = jnp.where(
                part_of == 0,
                pair(top_hi[here]),
                jnp.where(part_of == 1, pair(top_lo[here]), jnp.where(part_of == 2, pair(den_hi[here]), pair(den_lo[here]))),
            )
            both = jnp.concatenate([numer.reshape(n, 8, W), stats.reshape(n, 8, W)], axis=1).astype(BF16)
            if k:
                back_s[n * k : n * (k + 1)] = both
            else:
                back_s[1:n] = both[1:n]
                back[0] = both[0]

    returned = None
    reach = [min(k, n - k) for k in range(n)]
    low = max(1, n * 3 // 8)
    high = max(low + 1, n * 6 // 8)

    def part_at(k):
        return 0 if k < low else 1 if k < high else 2

    batches = BATCHES8 if n == 8 else (tuple(range(n)),)
    for batch in batches:
        for k in batch:
            if k:
                got2[k].wait_recv()
        attend(batch)
        pairs = [(k, j) for k in batch for j in range(n) if k or j]
        for k, j in sorted(pairs, key=lambda p: -reach[p[0]] - reach[p[1]]):
            slot = n * k + j
            send(back_s.at[slot], back.at[slot], bs_sem, br_sem.at[part_at(k)], plane(-k, -j), False)
    loads[11].wait()
    for copy in sends:
        copy.wait_send()
    sends.clear()
    lead = lax.rem(lane8, HD) < 16

    def spread(x):
        x = x + pltpu.roll(x, 16, x.ndim - 1)
        return x + pltpu.roll(x, 32, x.ndim - 1)

    def merge(spans):
        parts = []
        for which, begin, end in spans:
            if begin < end:
                here = pl.ds(max(begin, 1), end - max(begin, 1))
                pltpu.make_async_copy(back.at[here], back.at[here], br_sem.at[which]).wait()
                parts.append(back[begin:end].astype(F32))
        pieces = jnp.concatenate(parts, axis=0)
        count = pieces.shape[0]
        pieces = pieces.reshape(count, 2, 8, W)
        stats = pieces[:, 1].reshape(count * 8, W)
        stats = stats + pltpu.roll(stats, W - 16, 1)
        top = jnp.where(lead, jnp.max(stats.reshape(count, 8, W), axis=0), 0.0)
        factor = jnp.where(lead[None], jnp.exp(stats.reshape(count, 8, W) - top[None]), 0.0)
        factor = spread(factor.reshape(count * 8, W))
        numer = jnp.sum((pieces[:, 0].reshape(count * 8, W) * factor).reshape(count, 8, W), axis=0)
        denom = jnp.sum((stats * factor).reshape(count, 8, W), axis=0)
        return top, numer, denom

    near_top, near_numer, near_denom = merge([(0, 0, low * n), (2, high * n, n * n)])
    far_top, far_numer, far_denom = merge([(1, low * n, high * n)])
    top = jnp.where(lead, jnp.maximum(jnp.maximum(near_top, far_top), own), 0.0)
    near_factor = spread(jnp.where(lead, jnp.exp(near_top - top), 0.0))
    far_factor = spread(jnp.where(lead, jnp.exp(far_top - top), 0.0))
    numer = near_numer * near_factor + far_numer * far_factor
    denom = near_denom * near_factor + far_denom * far_factor
    top = spread(top)
    denom = jnp.where((lax.rem(lane8, HD) >= 32) & (lax.rem(lane8, HD) < 48), denom, 0.0)
    denom = denom + pltpu.roll(denom, 16, 1)
    denom = denom + pltpu.roll(denom, W - 32, 1)
    own_weight = jnp.exp(own - top)
    denom = denom + own_weight
    numer = numer + own_weight.astype(BF16).astype(F32) * v8
    attended = (numer / denom).astype(BF16).astype(F32)
    attended = jnp.concatenate([jnp.where(upper, attended, 0.0), jnp.where(upper, 0.0, attended)], axis=1)
    part = dot(attended.astype(BF16), wo[...])
    part = part + pltpu.roll(part, RD, 0)
    for k in range(heads_n):
        xs[k] = tile_of(part[:, 2 * W * k : 2 * W * (k + 1)])
    got5 = {
        k: send(xs.at[(hd + k) % heads_n], xr.at[k], xs_sem.at[k], xr_sem.at[k], along_x(k)) for k in xorder
    }
    others = pl.ds(1, n * n - 1)
    pltpu.make_async_copy(back_s.at[others], back.at[others], bs_sem).wait()
    summed = xs[hd]
    for k in range(1, heads_n):
        got5[k].wait_recv()
        summed = summed + xr[k]
    summed = (summed + res[hd]).astype(BF16)
    outs[0, :, 0:W] = summed[0:RD]
    outs[0, :, W : 2 * W] = summed[RD : 2 * RD]
    for copy in sends:
        copy.wait_send()


def shards(
    hidden_in,
    norm_gain,
    w_query,
    w_key,
    w_value,
    w_out,
    cache_keys,
    cache_values,
    block_node,
    block_len,
    live_count,
    node_parent,
    request_leaf,
):
    side = math.isqrt(lax.axis_size("blk") // 2)
    heads_n = lax.axis_size("head")
    d_model = hidden_in.shape[1]
    cols = w_query.shape[1]
    n = side
    rows = n * 2 * RD
    lanes = 2 * rows
    nodes = -(-node_parent.shape[0] // W) * W
    vmem = pl.BlockSpec(memory_space=pltpu.VMEM)
    hbm = pl.BlockSpec(memory_space=pltpu.HBM)
    shape = jax.ShapeDtypeStruct
    new = shape((3, RD, cols), BF16)
    dma = pltpu.SemaphoreType.DMA
    packed = pl.pallas_call(
        functools.partial(kernel, side, heads_n),
        out_shape=new,
        in_specs=[pl.BlockSpec(memory_space=pltpu.SMEM)] + [hbm] * 12,
        out_specs=vmem,
        scratch_shapes=[
            pltpu.VMEM((RD, d_model), BF16),
            pltpu.VMEM((1, d_model), F32),
            pltpu.VMEM((1, node_parent.shape[0]), jnp.int32),
            pltpu.VMEM((1, request_leaf.shape[0]), jnp.int32),
            pltpu.VMEM((1, SL), jnp.int32),
            pltpu.VMEM((1, SL), jnp.int32),
            pltpu.VMEM((d_model, cols), BF16),
            pltpu.VMEM((d_model, cols), BF16),
            pltpu.VMEM((d_model, cols), BF16),
            pltpu.VMEM((cols, d_model), BF16),
            pltpu.VMEM((2 * SL, BT, cols), BF16),
            pltpu.VMEM((2 * SL, BT, cols), BF16),
            pltpu.VMEM((2 * RD, d_model), F32),
            pltpu.VMEM((n, 2 * RD, W), F32),
            pltpu.VMEM((n, rows, W), BF16),
            pltpu.VMEM((8, W), F32),
            pltpu.VMEM((8, W), F32),
            pltpu.VMEM((1, nodes), F32),
            pltpu.VMEM((n * rows, request_leaf.shape[0]), BF16),
            pltpu.VMEM((n, rows, 2 * SL * BT), F32),
            pltpu.VMEM((n * n, 16, W), BF16),
            pltpu.VMEM((n * n, 16, W), BF16),
            pltpu.VMEM((heads_n, 8, W), F32),
            pltpu.VMEM((heads_n, 8, W), F32),
            pltpu.VMEM((heads_n, 8, W), F32),
            dma((12,)),
            dma((3,)),
            dma((3,)),
        ]
        + [dma((n,))] * 4
        + [dma(()), dma((3,))]
        + [dma((heads_n,))] * 2,
        compiler_params=pltpu.CompilerParams(
            collective_id=0, has_side_effects=True, vmem_limit_bytes=48 * 1024 * 1024
        ),
    )(
        live_count,
        *(
            pltpu.with_memory_space_constraint(x, pltpu.HBM)
            for x in (
                hidden_in,
                norm_gain.reshape(1, -1),
                node_parent.reshape(1, -1),
                request_leaf.reshape(1, -1),
                block_node.reshape(1, -1),
                block_len.reshape(1, -1),
                w_query,
                w_key,
                w_value,
                w_out,
                cache_keys,
                cache_values,
            )
        )
    )

    return packed[0], packed[1], packed[2]


def solution(mesh):
    in_specs = (
        P("blk", None),
        P(),
        P(None, "head"),
        P(None, "head"),
        P(None, "head"),
        P("head", None),
        P("blk", None, "head"),
        P("blk", None, "head"),
        P("blk"),
        P("blk"),
        P("blk"),
        P(),
        P(),
    )
    out_specs = (P("blk", "head"), P("blk", "head"), P("blk", "head"))
    return jax.shard_map(shards, mesh=mesh, in_specs=in_specs, out_specs=out_specs, check_vma=False)
```

```python
import functools
import math

import jax
import jax.numpy as jnp
from jax import lax
from jax.experimental import pallas as pl
from jax.experimental.pallas import tpu as pltpu
from jax.sharding import PartitionSpec as P

HD = 64
RD = 4
BT = 128
SL = 2
W = 128
MESH = pl.DeviceIdType.MESH
F32 = jnp.float32
BF16 = jnp.bfloat16

very_low = -1e30
low_top = -1e29
BATCHES8 = ((0,), (1, 7), (2, 6), (3, 5, 4))


def iota(shape, axis):
    return lax.broadcasted_iota(jnp.int32, shape, axis)


def dot_nt(a, b):
    return lax.dot_general(a, b, (((1,), (1,)), ((), ())), preferred_element_type=F32)


def dot(a, b):
    return jnp.dot(a, b, preferred_element_type=F32)


def kernel(
    side,
    heads_n,
    live,
    hidden_h,
    gain_h,
    parent_h,
    leaf_h,
    node_h,
    len_h,
    wq_h,
    wk_h,
    wv_h,
    wo_h,
    ck_h,
    cv_h,
    outs,
    hidden,
    gain,
    parent,
    leaf,
    node,
    length,
    wq,
    wk,
    wv,
    wo,
    kbuf,
    vbuf,
    hid8,
    g1,
    g2,
    meta_send,
    meta_recv,
    par,
    pick,
    bias,
    back_s,
    back,
    xs,
    xr,
    res,
    lsem,
    csem,
    crem,
    g1s_sem,
    g1r_sem,
    g2s_sem,
    g2r_sem,
    bs_sem,
    br_sem,
    xs_sem,
    xr_sem,
):
    n = side
    rows = n * 2 * RD
    lanes = 2 * rows
    nodes = par.shape[1]
    total = leaf.shape[1]
    me = lax.axis_index("blk")
    hd = lax.axis_index("head")
    core = me % 2
    y = (me // 2) % n
    z = me // (2 * n)
    flip = 1 - core
    a = y * flip + z * core
    b = z * flip + y * core

    step_a = 2 * flip + 2 * n * core
    step_b = 2 * n * flip + 2 * core
    base_a = [(a + k) % n * step_a + core for k in range(n)]
    base_b = [(b + k) % n * step_b for k in range(n)]

    def plane(k, j):
        return {"blk": base_a[k % n] + base_b[j % n], "head": hd}

    def along_a(k):
        return plane(k, 0)

    def along_b(k):
        return plane(0, k)

    def along_x(k):
        return {"blk": me, "head": (hd + k) % heads_n}

    other = {"blk": me + 1 - 2 * core, "head": hd}

    order = sorted(range(1, n), key=lambda k: -min(k, n - k))
    xorder = sorted(range(1, heads_n), key=lambda k: -min(k, heads_n - k))
    loads = [
        pltpu.make_async_copy(src, dst, lsem.at[k])
        for k, (src, dst) in enumerate(
            [
                (hidden_h, hidden),
                (gain_h, gain),
                (wq_h, wq),
                (node_h, node),
                (len_h, length),
                (wk_h, wk),
                (wv_h, wv),
                (cv_h, vbuf.at[pl.ds(0, SL)]),
                (ck_h, kbuf.at[pl.ds(0, SL)]),
                (parent_h, parent),
                (leaf_h, leaf),
                (wo_h, wo),
            ]
        )
    ]
    for load in loads[:3]:
        load.start()

    barrier = pltpu.get_barrier_semaphore()
    for k in order:
        pl.semaphore_signal(barrier, inc=1, device_id=along_b(k), device_id_type=MESH)
    for k in order:
        pl.semaphore_signal(barrier, inc=1, device_id=along_a(k), device_id_type=MESH)
    pl.semaphore_signal(barrier, inc=1, device_id=other, device_id_type=MESH)
    for k in xorder:
        pl.semaphore_signal(barrier, inc=1, device_id=along_x(k), device_id_type=MESH)
    for load in loads[3:]:
        load.start()

    loads[0].wait()
    loads[1].wait()
    states = hidden[...].astype(F32)
    hid8[pl.ds(0, RD), :] = states
    hid8[pl.ds(RD, RD), :] = states
    h8 = hid8[...]
    inv = lax.rsqrt(jnp.mean(h8 * h8, axis=1, keepdims=True) + 1e-06)
    normed = (h8 * inv * gain[...]).astype(BF16)
    row8 = iota((2 * RD, W), 0)
    lane8 = iota((2 * RD, W), 1)
    upper = row8 < RD

    def tile_of(wide):
        return jnp.where(upper, wide[:, 0:W], wide[:, W : 2 * W])

    loads[2].wait()
    q8 = tile_of(dot(normed, wq[...]).astype(BF16).astype(F32))
    g1[0] = q8

    for k in (3, 4):
        loads[k].wait()
    own_len = [jnp.where(s < live[0], length[:, s : s + 1], 0).astype(F32) for s in range(SL)]
    own_node = [node[:, s : s + 1].astype(F32) for s in range(SL)]

    def slot_tile(first):
        tile = jnp.zeros((8, W), F32)
        for s in range(SL):
            tile = jnp.where(row8 == first + s, own_node[s], tile)
            tile = jnp.where(row8 == 4 + first + s, own_len[s], tile)
        return tile

    meta_send[...] = slot_tile(SL)

    sends = []

    def send(src, dst, send_sem, recv_sem, target, alone=True):
        copy = pltpu.make_async_remote_copy(
            src_ref=src,
            dst_ref=dst,
            send_sem=send_sem,
            recv_sem=recv_sem,
            device_id=target,
            device_id_type=MESH,
        )
        copy.start()
        if alone:
            sends.append(copy)
        return copy

    pl.semaphore_wait(barrier, 2 * (n - 1) + 1 + heads_n - 1)

    got1 = {k: send(g1.at[0], g1.at[k], g1s_sem.at[k], g1r_sem.at[k], along_b(k)) for k in order}
    got_meta = send(meta_send, meta_recv, csem.at[0], crem.at[0], other)
    got_v = send(cv_h, vbuf.at[pl.ds(SL, SL)], csem.at[1], crem.at[1], other)
    got_k = send(ck_h, kbuf.at[pl.ds(SL, SL)], csem.at[2], crem.at[2], other)

    loads[5].wait()
    k8 = dot(normed, wk[...]).astype(BF16)
    outs[1] = k8[0:RD, :]
    loads[6].wait()
    v8 = dot(normed, wv[...]).astype(BF16)
    outs[2] = v8[0:RD, :]
    k8 = tile_of(k8.astype(F32))
    v8 = tile_of(v8.astype(F32))
    prod = q8 * k8
    left = lane8 < HD
    own = jnp.where(
        left,
        jnp.sum(jnp.where(left, prod, 0.0), axis=1, keepdims=True),
        jnp.sum(jnp.where(left, 0.0, prod), axis=1, keepdims=True),
    )
    for k in range(heads_n):
        res[k] = tile_of(h8[:, 2 * W * k : 2 * W * (k + 1)])

    spot = iota((n * rows, 1), 0)
    at_i = lax.rem(a + n - spot // rows, n)
    at_j = lax.rem(b + n - lax.rem(spot // (2 * RD), n), n)
    at_z = at_j * flip + at_i * core
    at_y = at_i * flip + at_j * core
    request = ((at_z * n + at_y) * 2 + core) * RD + lax.rem(spot, RD)
    pick[...] = jnp.where(iota((1, total), 1) == request, 1.0, 0.0).astype(BF16)

    for k in range(1, n):
        got1[k].wait_recv()
    g2[0] = g1[...].reshape(rows, W).astype(BF16)
    got2 = {k: send(g2.at[0], g2.at[k], g2s_sem.at[k], g2r_sem.at[k], along_a(k)) for k in order}

    loads[9].wait()
    loads[10].wait()
    par[...] = jnp.full_like(par, -1.0)
    par[:, 0 : parent.shape[1]] = parent[...].astype(F32)
    node_of_row = iota((nodes, 1), 0).astype(F32)
    hop = jnp.where(node_of_row == par[...], 1.0, 0.0).astype(BF16)
    leaf_hot = jnp.where(node_of_row == leaf[...].astype(F32), 1.0, 0.0).astype(BF16)
    got_meta.wait_recv()
    slots = slot_tile(0) + meta_recv[...]
    slot_node = jnp.concatenate([slots] * (nodes // W), axis=1)
    slot_len = jnp.concatenate([pltpu.roll(slots, 4, 0)] * (nodes // W), axis=1)
    level = jnp.where(iota((8, nodes), 1).astype(F32) == slot_node, 1.0, 0.0)
    up1 = dot(level.astype(BF16), hop)
    up2 = dot(up1.astype(BF16), hop)
    seen = dot((level + up1 + up2).astype(BF16), leaf_hot)
    row_of = iota((8, total), 0)
    unseen = jnp.where(row_of < 2 * SL, 1.0 - seen, jnp.where(row_of == 2 * SL, 1.0, 0.0))
    unseen = jnp.concatenate([unseen, jnp.zeros((W - 8, total), F32)], axis=0).astype(BF16)
    unseen = dot_nt(pick[...], unseen).astype(BF16)
    spot1 = iota((1, BT), 1).astype(F32)
    ends = [jnp.where(spot1 < slots[4 + s : 5 + s, :], 0.0, very_low) for s in range(2 * SL)]
    ends = jnp.concatenate(ends, axis=1)
    tokens = 2 * SL * BT
    slot_row = iota((W, tokens), 0)
    hide = jnp.where(
        slot_row == 2 * SL,
        ends,
        jnp.where(slot_row == iota((W, tokens), 1) // BT, very_low, 0.0),
    ).astype(BF16)
    bias[...] = dot(unseen, hide).reshape(n, rows, tokens)

    loads[7].wait()
    got_v.wait_recv()
    values = vbuf[...].reshape(tokens, 2 * W)
    loads[8].wait()
    got_k.wait_recv()
    keys = kbuf[...].reshape(tokens, 2 * W)

    spread_row = iota((lanes, 2 * W), 0)
    spread_lane = iota((lanes, 2 * W), 1)
    spread = jnp.where(
        (spread_row // rows == lax.rem(spread_lane // HD, 2)) & (lax.rem(spread_row // RD, 2) == spread_lane // W),
        1.0,
        0.0,
    ).astype(BF16)
    low_half = lax.rem(iota((lanes, W), 0), 2 * RD) < RD
    lane = iota((rows, W), 1)
    first = lane < HD
    part_of = lax.rem(lane, HD) // 16

    def pair(x):
        return jnp.where(first, x[0:rows], x[rows : 2 * rows])

    def split(x):
        hi = x.astype(BF16).astype(F32)
        return hi, (x - hi).astype(BF16).astype(F32)

    def attend(batch):
        queries, hidden_bias = [], []
        for k in batch:
            block = g2[k]
            block = jnp.concatenate([block, block], axis=1)
            queries.append(jnp.concatenate([block, block], axis=0) * spread)
            hidden_bias += [bias[k], bias[k]]
        scores = dot_nt(jnp.concatenate(queries, axis=0), keys) + jnp.concatenate(hidden_bias, axis=0)
        top_hi, top_lo = split(jnp.maximum(jnp.max(scores, axis=1, keepdims=True), low_top))
        weights = jnp.exp(scores - (top_hi + top_lo))
        den_hi, den_lo = split(jnp.sum(weights, axis=1, keepdims=True))
        full = dot(weights.astype(BF16), values)
        for at, k in enumerate(batch):
            here = slice(at * lanes, (at + 1) * lanes)
            numer = pair(jnp.where(low_half, full[here, 0:W], full[here, W : 2 * W]))
            stats = jnp.where(
                part_of == 0,
                pair(top_hi[here]),
                jnp.where(part_of == 1, pair(top_lo[here]), jnp.where(part_of == 2, pair(den_hi[here]), pair(den_lo[here]))),
            )
            both = jnp.concatenate([numer.reshape(n, 8, W), stats.reshape(n, 8, W)], axis=1).astype(BF16)
            if k:
                back_s[n * k : n * (k + 1)] = both
            else:
                back_s[1:n] = both[1:n]
                back[0] = both[0]

    returned = None
    reach = [min(k, n - k) for k in range(n)]
    low = max(1, n * 3 // 8)
    high = max(low + 1, n * 6 // 8)

    def part_at(k):
        return 0 if k < low else 1 if k < high else 2

    batches = BATCHES8 if n == 8 else (tuple(range(n)),)
    for batch in batches:
        for k in batch:
            if k:
                got2[k].wait_recv()
        attend(batch)
        pairs = [(k, j) for k in batch for j in range(n) if k or j]
        for k, j in sorted(pairs, key=lambda p: -reach[p[0]] - reach[p[1]]):
            slot = n * k + j
            send(back_s.at[slot], back.at[slot], bs_sem, br_sem.at[part_at(k)], plane(-k, -j), False)
    loads[11].wait()
    for copy in sends:
        copy.wait_send()
    sends.clear()
    lead = lax.rem(lane8, HD) < 16

    def spread(x):
        x = x + pltpu.roll(x, 16, x.ndim - 1)
        return x + pltpu.roll(x, 32, x.ndim - 1)

    def merge(spans):
        parts = []
        for which, begin, end in spans:
            if begin < end:
                here = pl.ds(max(begin, 1), end - max(begin, 1))
                pltpu.make_async_copy(back.at[here], back.at[here], br_sem.at[which]).wait()
                parts.append(back[begin:end].astype(F32))
        pieces = jnp.concatenate(parts, axis=0)
        count = pieces.shape[0]
        pieces = pieces.reshape(count, 2, 8, W)
        stats = pieces[:, 1].reshape(count * 8, W)
        stats = stats + pltpu.roll(stats, W - 16, 1)
        top = jnp.where(lead, jnp.max(stats.reshape(count, 8, W), axis=0), 0.0)
        factor = jnp.where(lead[None], jnp.exp(stats.reshape(count, 8, W) - top[None]), 0.0)
        factor = spread(factor.reshape(count * 8, W))
        numer = jnp.sum((pieces[:, 0].reshape(count * 8, W) * factor).reshape(count, 8, W), axis=0)
        denom = jnp.sum((stats * factor).reshape(count, 8, W), axis=0)
        return top, numer, denom

    near_top, near_numer, near_denom = merge([(0, 0, low * n), (2, high * n, n * n)])
    far_top, far_numer, far_denom = merge([(1, low * n, high * n)])
    top = jnp.where(lead, jnp.maximum(jnp.maximum(near_top, far_top), own), 0.0)
    near_factor = spread(jnp.where(lead, jnp.exp(near_top - top), 0.0))
    far_factor = spread(jnp.where(lead, jnp.exp(far_top - top), 0.0))
    numer = near_numer * near_factor + far_numer * far_factor
    denom = near_denom * near_factor + far_denom * far_factor
    top = spread(top)
    denom = jnp.where((lax.rem(lane8, HD) >= 32) & (lax.rem(lane8, HD) < 48), denom, 0.0)
    denom = denom + pltpu.roll(denom, 16, 1)
    denom = denom + pltpu.roll(denom, W - 32, 1)
    own_weight = jnp.exp(own - top)
    denom = denom + own_weight
    numer = numer + own_weight.astype(BF16).astype(F32) * v8
    attended = (numer / denom).astype(BF16).astype(F32)
    attended = jnp.concatenate([jnp.where(upper, attended, 0.0), jnp.where(upper, 0.0, attended)], axis=1)
    part = dot(attended.astype(BF16), wo[...])
    part = part + pltpu.roll(part, RD, 0)
    for k in range(heads_n):
        xs[k] = tile_of(part[:, 2 * W * k : 2 * W * (k + 1)])
    got5 = {
        k: send(xs.at[(hd + k) % heads_n], xr.at[k], xs_sem.at[k], xr_sem.at[k], along_x(k)) for k in xorder
    }
    others = pl.ds(1, n * n - 1)
    pltpu.make_async_copy(back_s.at[others], back.at[others], bs_sem).wait()
    summed = xs[hd]
    for k in range(1, heads_n):
        got5[k].wait_recv()
        summed = summed + xr[k]
    summed = (summed + res[hd]).astype(BF16)
    outs[0, :, 0:W] = summed[0:RD]
    outs[0, :, W : 2 * W] = summed[RD : 2 * RD]
    for copy in sends:
        copy.wait_send()


def shards(
    hidden_in,
    norm_gain,
    w_query,
    w_key,
    w_value,
    w_out,
    cache_keys,
    cache_values,
    block_node,
    block_len,
    live_count,
    node_parent,
    request_leaf,
):
    side = math.isqrt(lax.axis_size("blk") // 2)
    heads_n = lax.axis_size("head")
    d_model = hidden_in.shape[1]
    cols = w_query.shape[1]
    n = side
    rows = n * 2 * RD
    lanes = 2 * rows
    nodes = -(-node_parent.shape[0] // W) * W
    vmem = pl.BlockSpec(memory_space=pltpu.VMEM)
    hbm = pl.BlockSpec(memory_space=pltpu.HBM)
    shape = jax.ShapeDtypeStruct
    new = shape((3, RD, cols), BF16)
    dma = pltpu.SemaphoreType.DMA
    packed = pl.pallas_call(
        functools.partial(kernel, side, heads_n),
        out_shape=new,
        in_specs=[pl.BlockSpec(memory_space=pltpu.SMEM)] + [hbm] * 12,
        out_specs=vmem,
        scratch_shapes=[
            pltpu.VMEM((RD, d_model), BF16),
            pltpu.VMEM((1, d_model), F32),
            pltpu.VMEM((1, node_parent.shape[0]), jnp.int32),
            pltpu.VMEM((1, request_leaf.shape[0]), jnp.int32),
            pltpu.VMEM((1, SL), jnp.int32),
            pltpu.VMEM((1, SL), jnp.int32),
            pltpu.VMEM((d_model, cols), BF16),
            pltpu.VMEM((d_model, cols), BF16),
            pltpu.VMEM((d_model, cols), BF16),
            pltpu.VMEM((cols, d_model), BF16),
            pltpu.VMEM((2 * SL, BT, cols), BF16),
            pltpu.VMEM((2 * SL, BT, cols), BF16),
            pltpu.VMEM((2 * RD, d_model), F32),
            pltpu.VMEM((n, 2 * RD, W), F32),
            pltpu.VMEM((n, rows, W), BF16),
            pltpu.VMEM((8, W), F32),
            pltpu.VMEM((8, W), F32),
            pltpu.VMEM((1, nodes), F32),
            pltpu.VMEM((n * rows, request_leaf.shape[0]), BF16),
            pltpu.VMEM((n, rows, 2 * SL * BT), F32),
            pltpu.VMEM((n * n, 16, W), BF16),
            pltpu.VMEM((n * n, 16, W), BF16),
            pltpu.VMEM((heads_n, 8, W), F32),
            pltpu.VMEM((heads_n, 8, W), F32),
            pltpu.VMEM((heads_n, 8, W), F32),
            dma((12,)),
            dma((3,)),
            dma((3,)),
        ]
        + [dma((n,))] * 4
        + [dma(()), dma((3,))]
        + [dma((heads_n,))] * 2,
        compiler_params=pltpu.CompilerParams(
            collective_id=0, has_side_effects=True, vmem_limit_bytes=48 * 1024 * 1024
        ),
    )(
        live_count,
        *(
            pltpu.with_memory_space_constraint(x, pltpu.HBM)
            for x in (
                hidden_in,
                norm_gain.reshape(1, -1),
                node_parent.reshape(1, -1),
                request_leaf.reshape(1, -1),
                block_node.reshape(1, -1),
                block_len.reshape(1, -1),
                w_query,
                w_key,
                w_value,
                w_out,
                cache_keys,
                cache_values,
            )
        )
    )

    return packed[0], packed[1], packed[2]


def solution(mesh):
    in_specs = (
        P("blk", None),
        P(),
        P(None, "head"),
        P(None, "head"),
        P(None, "head"),
        P("head", None),
        P("blk", None, "head"),
        P("blk", None, "head"),
        P("blk"),
        P("blk"),
        P("blk"),
        P(),
        P(),
    )
    out_specs = (P("blk", "head"), P("blk", "head"), P("blk", "head"))
    return jax.shard_map(shards, mesh=mesh, in_specs=in_specs, out_specs=out_specs, check_vma=False)
```
